32 devices in a mesh: dp: 8 (over z, x), tensor: 4 (over y, core).
Axes of the slice: x: 2, y: 2, z: 4, core: 2. Of those that a mesh axis runs over, the one named last changes fastest.
Arguments:
- hidden_input: bfloat16 [4, 4096, 14336], P(None, 'dp', 'tensor'), may hold values from -6 to 6
- out_cotangent: bfloat16 [4, 4096, 4096], P(None, 'dp', 'tensor'), may hold values from -6 to 6
- in_projection: bfloat16 [4, 64, 14336], P(None, None, 'tensor'), may hold values from -0.046875 to 0.046875
- out_projection: bfloat16 [4, 64, 4096], P(None, None, 'tensor'), may hold values from -0.09375 to 0.09375
- forget_grads: bfloat16 [1024, 16384], P('dp', 'tensor'), may hold values from -0.001953125 to 0.001953125
Outputs:
- attribution_scores: float32 [8, 1024], P('dp')
The draws below stay inside these ranges and needn't reach their ends.
All inputs are finite; a program needn't handle non-finite values.
Results may differ from the reference program's by a relative error of at most 0.0029.
Values may be sent and summed in bfloat16 or wider, within the bound.
No kernel may reach another device: no remote copies, remote signals or barrier semaphores. Data moves between devices by JAX's collectives and lax.ppermute only.
A program may use at most 128 MiB of HBM per device.

```python
import jax
import jax.numpy as jnp
from jax import lax

D = 4096
FF = 14336
RANK = 64
LAYERS = 4
SEQ = 512
TOKENS = 4096
FORGET = 1024
PROJ = 16384


def block_scale(rng, dims, shards, low, largest):
    loudness, own = 1.0, jax.random.fold_in(rng, 6)
    for dim, blocks in shards:
        steps = jnp.exp(jax.random.uniform(jax.random.fold_in(own, dim), (blocks,), jnp.float32, low / len(shards), largest / len(shards)))
        loudness = loudness * jnp.repeat(steps, dims[dim] // blocks).reshape([-1 if axis == dim else 1 for axis in range(len(dims))])
    return loudness


def noise(own_key, dims, spread, reach, pieces=(), kind=jnp.bfloat16):
    values = jax.random.normal(own_key, dims, jnp.float32) * spread
    if len(pieces) > 0:
        values = block_scale(own_key, dims, pieces, -0.22, 0.18) * values
    return jnp.clip(values, min=-reach, max=reach).astype(kind)


def setup_inputs(seed: int = 0) -> dict:
    arg_keys = jax.random.split(jax.random.key(seed), 6)
    return {
        "hidden_input": noise(arg_keys[0], (LAYERS, TOKENS, FF), 1.0, 6.0, ((1, 8), (2, 4))),
        "out_cotangent": noise(arg_keys[1], (LAYERS, TOKENS, D), 1.0, 6.0, ((1, 8), (2, 4))),
        "in_projection": noise(arg_keys[2], (LAYERS, RANK, FF), FF ** -0.5, 0.046875, ((2, 4),)),
        "out_projection": noise(arg_keys[3], (LAYERS, RANK, D), D ** -0.5, 0.09375, ((2, 4),)),
        "forget_grads": noise(arg_keys[4], (FORGET, PROJ), (SEQ * PROJ) ** -0.5, 0.001953125, ((0, 8), (1, 4))),
    }


def reference(hidden_input, out_cotangent, in_projection, out_projection, forget_grads):
    doc_count = hidden_input.shape[1] // SEQ
    blocks = []
    for layer_idx in range(LAYERS):
        in_coords = jnp.dot(hidden_input[layer_idx], in_projection[layer_idx].T, preferred_element_type=jnp.float32)
        out_coords = jnp.dot(out_cotangent[layer_idx], out_projection[layer_idx].T, preferred_element_type=jnp.float32)
        per_layer = jnp.einsum("dsr,dsc->drc", out_coords.reshape(doc_count, SEQ, RANK), in_coords.reshape(doc_count, SEQ, RANK), precision=lax.Precision.HIGHEST)
        blocks.append(per_layer.reshape(doc_count, RANK * RANK))
    per_example = jnp.concatenate(blocks, axis=1).astype(jnp.bfloat16)
    return jnp.dot(per_example, forget_grads.T, preferred_element_type=jnp.float32)
```

```python
import functools

import jax
import jax.numpy as jnp
from jax import lax
from jax.experimental import pallas as pl
from jax.experimental.pallas import tpu as pltpu
from jax.sharding import PartitionSpec as P

SEQ = 512
VMEM_LIMIT = 20 * 1024 * 1024


def coords_kernel(flips, hid, cot, inp, outp, *rest):
    n = len(flips)
    outs = rest[:n]
    hbuf, cbuf, ibuf, obuf, acc, hsem, csem, isem, osem = rest[n:]
    rank = inp.shape[1]
    chunks, wide = hbuf.shape[1], hbuf.shape[3]
    me = lax.axis_index("tensor")

    def out_copies(s, layer):
        return (
            pltpu.make_async_copy(outp.at[layer], obuf.at[s, pl.ds(0, rank)], osem.at[s]),
            pltpu.make_async_copy(cot.at[layer], cbuf.at[s], csem.at[s]),
            pltpu.make_async_copy(inp.at[layer], ibuf.at[s, pl.ds(rank, rank)], isem.at[s]),
        )

    def hid_copy(s, layer, c):
        part = pl.ds(pl.multiple_of(c * wide, 128), wide)
        return pltpu.make_async_copy(hid.at[layer, :, part], hbuf.at[s, c], hsem.at[s, c])

    for s, flip in enumerate(flips):
        layer = lax.bitwise_xor(me, flip)
        for copy in out_copies(s, layer):
            copy.start()
        for c in range(chunks):
            hid_copy(s, layer, c).start()
    obuf[:, rank:, :] = jnp.zeros((n, rank, obuf.shape[2]), obuf.dtype)
    ibuf[:, :rank, :] = jnp.zeros((n, rank, ibuf.shape[2]), ibuf.dtype)
    dims = (((1,), (1,)), ((), ()))

    @pl.loop(0, n)
    def _(s):
        for copy in out_copies(s, 0):
            copy.wait()
        acc[s] = lax.dot_general(cbuf[s], obuf[s], dims, preferred_element_type=jnp.float32)

        @pl.loop(0, chunks)
        def _(c):
            hid_copy(s, 0, c).wait()
            part = pl.ds(pl.multiple_of(c * wide, 128), wide)
            acc[s] += lax.dot_general(
                hbuf[s, c], ibuf[s, :, part], dims, preferred_element_type=jnp.float32
            )

    for s in range(n):
        outs[s][...] = acc[s]


def coords(flips, hid, cot, inp, outp):
    n, chunks = len(flips), 2
    _, toks, width = hid.shape
    feats, rank = cot.shape[2], inp.shape[1]
    moved = n * (toks + rank) * (width + feats) * 2
    return pl.pallas_call(
        functools.partial(coords_kernel, flips),
        out_shape=[jax.ShapeDtypeStruct((toks, 2 * rank), jnp.float32)] * n,
        in_specs=[pl.BlockSpec(memory_space=pltpu.HBM)] * 4,
        out_specs=[pl.BlockSpec(memory_space=pltpu.VMEM)] * n,
        scratch_shapes=[
            pltpu.VMEM((n, chunks, toks, width // chunks), jnp.bfloat16),
            pltpu.VMEM((n, toks, feats), jnp.bfloat16),
            pltpu.VMEM((n, 2 * rank, width), jnp.bfloat16),
            pltpu.VMEM((n, 2 * rank, feats), jnp.bfloat16),
            pltpu.VMEM((n, toks, 2 * rank), jnp.float32),
            pltpu.SemaphoreType.DMA((n, chunks)),
            pltpu.SemaphoreType.DMA((n,)),
            pltpu.SemaphoreType.DMA((n,)),
            pltpu.SemaphoreType.DMA((n,)),
        ],
        compiler_params=pltpu.CompilerParams(vmem_limit_bytes=VMEM_LIMIT),
        cost_estimate=pl.CostEstimate(
            flops=2 * n * toks * rank * (width + feats), bytes_accessed=moved, transcendentals=0
        ),
    )(*(pltpu.with_memory_space_constraint(a, pltpu.HBM) for a in (hid, cot, inp, outp)))


def grad_kernel(rank, mine, core, chip, grad, tmp):
    total = mine[...] + core[...] + chip[...]
    square = lax.dot_general(
        total,
        total,
        (((0,), (0,)), ((), ())),
        precision=lax.Precision.HIGHEST,
        preferred_element_type=jnp.float32,
    )
    tmp[...] = square[:rank, rank:]
    even = tmp[pl.ds(0, rank // 2, stride=2), :]
    odd = tmp[pl.ds(1, rank // 2, stride=2), :]
    flat = jnp.concatenate([even, odd], axis=1).astype(grad.dtype)
    for d in range(grad.shape[0]):
        grad[d] = flat


def layer_grad(mine, core, chip, copies):
    rank = mine.shape[1] // 2
    vmem = pl.BlockSpec(memory_space=pltpu.VMEM)
    return pl.pallas_call(
        functools.partial(grad_kernel, rank),
        out_shape=jax.ShapeDtypeStruct((copies, rank // 2, 2 * rank), jnp.bfloat16),
        in_specs=[vmem] * 3,
        out_specs=vmem,
        scratch_shapes=[pltpu.VMEM((rank, rank), jnp.float32)],
        compiler_params=pltpu.CompilerParams(vmem_limit_bytes=8 * 1024 * 1024),
    )(mine, core, chip)


def one_layer_each(hidden_input, out_cotangent, in_projection, out_projection, forget_grads):
    docs, tensor = lax.axis_size("dp"), lax.axis_size("tensor")

    def swap(array, flip):
        return lax.ppermute(array, "tensor", [(i, i ^ flip) for i in range(tensor)])

    arrays = (hidden_input, out_cotangent, in_projection, out_projection)
    far_other, far_mine = coords((3, 2), *arrays)
    far_sum = far_mine + swap(far_other, 1)
    far_sum, *arrays = lax.optimization_barrier((far_sum, *arrays))
    chip = swap(far_sum, 2)
    near_other, mine = coords((1, 0), *arrays)
    core = swap(near_other, 1)
    grad = layer_grad(mine, core, chip, docs)
    grads = lax.all_to_all(grad, "dp", 0, 0, tiled=True)
    part = lax.dot_general(
        grads.reshape(docs, -1),
        forget_grads,
        (((1,), (1,)), ((), ())),
        preferred_element_type=jnp.float32,
    )
    rows = jnp.broadcast_to(part[:, None, None, :], (docs, tensor, 1, part.shape[1]))
    rows = rows.reshape(docs * tensor, 1, part.shape[1])
    rows = lax.all_to_all(rows, ("dp", "tensor"), 0, 0, tiled=True)
    return rows.reshape(docs, tensor, -1).sum(axis=1).reshape(1, -1)


def any_split(hidden_input, out_cotangent, in_projection, out_projection, forget_grads):
    docs_axis = lax.axis_size("dp")
    in_coords = jnp.einsum(
        "ltf,lrf->tlr", hidden_input, in_projection, preferred_element_type=jnp.float32
    )
    out_coords = jnp.einsum(
        "ltf,lrf->tlr", out_cotangent, out_projection, preferred_element_type=jnp.float32
    )
    toks, layers, rank = in_coords.shape
    docs = toks // SEQ
    out_coords, in_coords = lax.psum((out_coords, in_coords), "tensor")
    grads = jnp.einsum(
        "dslr,dslc->dlrc",
        out_coords.reshape(docs, SEQ, layers, rank),
        in_coords.reshape(docs, SEQ, layers, rank),
        precision=lax.Precision.HIGHEST,
    ).reshape(docs, layers * rank * rank)
    width = grads.shape[1] // lax.axis_size("tensor")
    grads = lax.dynamic_slice_in_dim(grads, lax.axis_index("tensor") * width, width, 1)
    grads = lax.all_gather(grads.astype(jnp.bfloat16), "dp", axis=0, tiled=True)
    part = lax.dot_general(
        grads, forget_grads, (((1,), (1,)), ((), ())), preferred_element_type=jnp.float32
    )
    part = lax.psum(part, "tensor").reshape(docs_axis, docs, -1)
    rows = lax.all_to_all(part, "dp", 0, 0, tiled=True)
    return rows.transpose(1, 0, 2).reshape(docs, -1)


def solution(mesh):
    in_specs = (
        P(None, "dp", "tensor"),
        P(None, "dp", "tensor"),
        P(None, None, "tensor"),
        P(None, None, "tensor"),
        P("dp", "tensor"),
    )

    def on_device(hidden_input, *others):
        layers, toks, _ = hidden_input.shape
        single = mesh.shape["tensor"] == layers == 4 and toks == SEQ
        return (one_layer_each if single else any_split)(hidden_input, *others)

    return jax.shard_map(
        on_device, mesh=mesh, in_specs=in_specs, out_specs=P("dp", None), check_vma=False
    )
```

```python
import functools

import jax
import jax.numpy as jnp
from jax import lax
from jax.experimental import pallas as pl
from jax.experimental.pallas import tpu as pltpu
from jax.sharding import PartitionSpec as P

SEQ = 512
VMEM_LIMIT = 20 * 1024 * 1024


def pieces(lo, hi, split):
    before = (lo, min(hi, split), 0) if lo < split else None
    after = (max(lo, split) - split, hi - split, max(lo, split) - lo) if hi > split else None
    return before, after


def coords_kernel(flips, hid, cot, inp, outp, *rest):
    n = len(flips)
    outs = rest[:n]
    xbuf, wbuf, acc, xsem, wsem = rest[n:]
    rank = inp.shape[1]
    chunks, wide = xbuf.shape[1], xbuf.shape[3]
    me = lax.axis_index("tensor")
    parts = [pieces(c * wide, (c + 1) * wide, hid.shape[2]) for c in range(chunks)]
    for s, flip in enumerate(flips):
        layer = lax.bitwise_xor(me, flip)
        for c, both in enumerate(parts):
            for part, x, w, row in zip(both, (hid, cot), (inp, outp), (rank, 0)):
                if part is None:
                    continue
                src, dst = pl.ds(part[0], part[1] - part[0]), pl.ds(part[2], part[1] - part[0])
                pltpu.make_async_copy(
                    w.at[layer, :, src], wbuf.at[s, c, pl.ds(row, rank), dst], wsem.at[s, c]
                ).start()
                pltpu.make_async_copy(
                    x.at[layer, :, src], xbuf.at[s, c, :, dst], xsem.at[s, c]
                ).start()
    for s in range(n):
        for c, both in enumerate(parts):
            for part, row in zip(both, (0, rank)):
                if part is not None:
                    size = part[1] - part[0]
                    wbuf[s, c, row : row + rank, part[2] : part[2] + size] = jnp.zeros(
                        (rank, size), wbuf.dtype
                    )
    acc[...] = jnp.zeros_like(acc)

    @pl.loop(0, n)
    def _(s):
        @pl.loop(0, chunks)
        def _(c):
            w_all = wbuf.at[s, c, pl.ds(0, rank)]
            pltpu.make_async_copy(w_all, w_all, wsem.at[s, c]).wait()
            x_all = xbuf.at[s, c]
            pltpu.make_async_copy(x_all, x_all, xsem.at[s, c]).wait()
            acc[s] += lax.dot_general(
                xbuf[s, c], wbuf[s, c], (((1,), (1,)), ((), ())), preferred_element_type=jnp.float32
            )

    for s in range(n):
        outs[s][...] = acc[s]


def coords(flips, hid, cot, inp, outp):
    n, chunks = len(flips), 2
    _, toks, width = hid.shape
    feats, rank = cot.shape[2], inp.shape[1]
    wide = (width + feats) // chunks
    return pl.pallas_call(
        functools.partial(coords_kernel, flips),
        out_shape=[jax.ShapeDtypeStruct((toks, 2 * rank), jnp.float32)] * n,
        in_specs=[pl.BlockSpec(memory_space=pltpu.HBM)] * 4,
        out_specs=[pl.BlockSpec(memory_space=pltpu.VMEM)] * n,
        scratch_shapes=[
            pltpu.VMEM((n, chunks, toks, wide), jnp.bfloat16),
            pltpu.VMEM((n, chunks, 2 * rank, wide), jnp.bfloat16),
            pltpu.VMEM((n, toks, 2 * rank), jnp.float32),
            pltpu.SemaphoreType.DMA((n, chunks)),
            pltpu.SemaphoreType.DMA((n, chunks)),
        ],
        compiler_params=pltpu.CompilerParams(vmem_limit_bytes=VMEM_LIMIT),
        cost_estimate=pl.CostEstimate(
            flops=2 * n * toks * rank * (width + feats),
            bytes_accessed=n * (toks + rank) * (width + feats) * 2,
            transcendentals=0,
        ),
    )(*(pltpu.with_memory_space_constraint(a, pltpu.HBM) for a in (hid, cot, inp, outp)))


def grad_kernel(rank, mine, core, chip, grad, tmp):
    total = mine[...] + core[...] + chip[...]
    square = lax.dot_general(
        total,
        total,
        (((0,), (0,)), ((), ())),
        precision=lax.Precision.HIGHEST,
        preferred_element_type=jnp.float32,
    )
    tmp[...] = square[:rank, rank:]
    even = tmp[pl.ds(0, rank // 2, stride=2), :]
    odd = tmp[pl.ds(1, rank // 2, stride=2), :]
    flat = jnp.concatenate([even, odd], axis=1).astype(grad.dtype)
    for d in range(grad.shape[0]):
        grad[d] = flat


def layer_grad(mine, core, chip, copies):
    rank = mine.shape[1] // 2
    vmem = pl.BlockSpec(memory_space=pltpu.VMEM)
    return pl.pallas_call(
        functools.partial(grad_kernel, rank),
        out_shape=jax.ShapeDtypeStruct((copies, rank // 2, 2 * rank), jnp.bfloat16),
        in_specs=[vmem] * 3,
        out_specs=vmem,
        scratch_shapes=[pltpu.VMEM((rank, rank), jnp.float32)],
        compiler_params=pltpu.CompilerParams(vmem_limit_bytes=8 * 1024 * 1024),
    )(mine, core, chip)


def one_layer_each(hidden_input, out_cotangent, in_projection, out_projection, forget_grads):
    docs, tensor = lax.axis_size("dp"), lax.axis_size("tensor")

    def swap(array, flip):
        return lax.ppermute(array, "tensor", [(i, i ^ flip) for i in range(tensor)])

    arrays = (hidden_input, out_cotangent, in_projection, out_projection)
    far_other, far_mine = coords((3, 2), *arrays)
    far_sum = far_mine + swap(far_other, 1)
    far_sum, *arrays = lax.optimization_barrier((far_sum, *arrays))
    chip = swap(far_sum, 2)
    near_other, mine = coords((1, 0), *arrays)
    core = swap(near_other, 1)
    grad = layer_grad(mine, core, chip, docs)
    grads = lax.all_to_all(grad, "dp", 0, 0, tiled=True)
    part = lax.dot_general(
        grads.reshape(docs, -1),
        forget_grads,
        (((1,), (1,)), ((), ())),
        preferred_element_type=jnp.float32,
    )
    rows = jnp.broadcast_to(part[:, None, None, :], (docs, tensor, 1, part.shape[1]))
    rows = rows.reshape(docs * tensor, 1, part.shape[1])
    rows = lax.all_to_all(rows, ("dp", "tensor"), 0, 0, tiled=True)
    return rows.reshape(docs, tensor, -1).sum(axis=1).reshape(1, -1)


def any_split(hidden_input, out_cotangent, in_projection, out_projection, forget_grads):
    docs_axis = lax.axis_size("dp")
    in_coords = jnp.einsum(
        "ltf,lrf->tlr", hidden_input, in_projection, preferred_element_type=jnp.float32
    )
    out_coords = jnp.einsum(
        "ltf,lrf->tlr", out_cotangent, out_projection, preferred_element_type=jnp.float32
    )
    toks, layers, rank = in_coords.shape
    docs = toks // SEQ
    out_coords, in_coords = lax.psum((out_coords, in_coords), "tensor")
    grads = jnp.einsum(
        "dslr,dslc->dlrc",
        out_coords.reshape(docs, SEQ, layers, rank),
        in_coords.reshape(docs, SEQ, layers, rank),
        precision=lax.Precision.HIGHEST,
    ).reshape(docs, layers * rank * rank)
    width = grads.shape[1] // lax.axis_size("tensor")
    grads = lax.dynamic_slice_in_dim(grads, lax.axis_index("tensor") * width, width, 1)
    grads = lax.all_gather(grads.astype(jnp.bfloat16), "dp", axis=0, tiled=True)
    part = lax.dot_general(
        grads, forget_grads, (((1,), (1,)), ((), ())), preferred_element_type=jnp.float32
    )
    part = lax.psum(part, "tensor").reshape(docs_axis, docs, -1)
    rows = lax.all_to_all(part, "dp", 0, 0, tiled=True)
    return rows.transpose(1, 0, 2).reshape(docs, -1)


def solution(mesh):
    in_specs = (
        P(None, "dp", "tensor"),
        P(None, "dp", "tensor"),
        P(None, None, "tensor"),
        P(None, None, "tensor"),
        P("dp", "tensor"),
    )

    def on_device(hidden_input, *others):
        layers, toks, _ = hidden_input.shape
        single = mesh.shape["tensor"] == layers == 4 and toks == SEQ
        return (one_layer_each if single else any_split)(hidden_input, *others)

    return jax.shard_map(
        on_device, mesh=mesh, in_specs=in_specs, out_specs=P("dp", None), check_vma=False
    )
```

```python
import functools

import jax
import jax.numpy as jnp
from jax import lax
from jax.experimental import pallas as pl
from jax.experimental.pallas import tpu as pltpu
from jax.sharding import PartitionSpec as P

SEQ = 512
VMEM_LIMIT = 20 * 1024 * 1024


def pieces(lo, hi, split):
    before = (lo, min(hi, split), 0) if lo < split else None
    after = (max(lo, split) - split, hi - split, max(lo, split) - lo) if hi > split else None
    return before, after


def coords_kernel(stage, *refs):
    flips, cut, after, loaded, fetch = stage
    n, refs = len(flips), list(refs)
    hid, cot, inp, outp = refs[:4]
    far = refs[4] if fetch else None
    refs = refs[4 + fetch + 2 * loaded :]
    outs, refs = refs[: n + cut - 1], refs[n + cut - 1 :]
    near, refs = (refs[0], refs[1:]) if fetch else (None, refs)
    nextx, nextw, refs = (refs[0], refs[1], refs[2:]) if after else (None, None, refs)
    xbuf, wbuf, acc, xsem, wsem, nsem, fsem = refs
    rank = inp.shape[1]
    wide = xbuf.shape[2]
    chunks = (hid.shape[2] + cot.shape[2]) // wide
    me = lax.axis_index("tensor")
    parts = [pieces(c * wide, (c + 1) * wide, hid.shape[2]) for c in range(chunks)]

    def load(flip, c, x_at, w_at, x_sem, w_sem):
        layer = lax.bitwise_xor(me, flip)
        for part, x, w, row in zip(parts[c], (hid, cot), (inp, outp), (rank, 0)):
            if part is not None:
                src, dst = pl.ds(part[0], part[1] - part[0]), pl.ds(part[2], part[1] - part[0])
                pltpu.make_async_copy(
                    w.at[layer, :, src], w_at.at[pl.ds(row, rank), dst], w_sem
                ).start()
                pltpu.make_async_copy(x.at[layer, :, src], x_at.at[:, dst], x_sem).start()

    def clear(c, w_at):
        for part, row in zip(parts[c], (0, rank)):
            if part is not None:
                size = part[1] - part[0]
                w_at[row : row + rank, part[2] : part[2] + size] = jnp.zeros((rank, size), w_at.dtype)

    def arrived(x_at, w_at, x_sem, w_sem):
        w_all = w_at.at[pl.ds(0, rank)]
        pltpu.make_async_copy(w_all, w_all, w_sem).wait()
        pltpu.make_async_copy(x_at, x_at, x_sem).wait()

    steps = [(flip, c) for flip in flips for c in range(chunks)]
    for t, (flip, c) in enumerate(steps):
        if t >= loaded:
            load(flip, c, xbuf.at[t], wbuf.at[t], xsem.at[t], wsem.at[t])
    if after:
        load(after[0], 0, nextx.at[0], nextw.at[0], nsem.at[0], nsem.at[1])
    if fetch:
        pltpu.make_async_copy(far, near, fsem).start()
    for t, (flip, c) in enumerate(steps):
        if t >= loaded:
            clear(c, wbuf.at[t])
    if after:
        clear(0, nextw.at[0])
    acc[...] = jnp.zeros_like(acc)

    @pl.loop(0, len(steps))
    def _(t):
        @pl.when(t >= loaded)
        def _():
            arrived(xbuf.at[t], wbuf.at[t], xsem.at[t], wsem.at[t])

        acc[t // chunks] += lax.dot_general(
            xbuf[t], wbuf[t], (((1,), (1,)), ((), ())), preferred_element_type=jnp.float32
        )

    for k in range(cut):
        rows = outs[k].shape[0]
        outs[k][...] = acc[0, k * rows : (k + 1) * rows]
    for s in range(1, n):
        outs[cut + s - 1][...] = acc[s]
    if after:
        arrived(nextx.at[0], nextw.at[0], nsem.at[0], nsem.at[1])
    if fetch:
        pltpu.make_async_copy(far, near, fsem).wait()


def coords(flips, arrays, cut=1, after=(), ready=(), far=()):
    hid, cot, inp, _ = arrays
    n, chunks = len(flips), 2
    _, toks, width = hid.shape
    feats, rank = cot.shape[2], inp.shape[1]
    wide = (width + feats) // chunks

    def buffers(layers, make):
        steps = layers * chunks
        return [make((steps, rows, wide), jnp.bfloat16) for rows in (toks, 2 * rank)]

    own = buffers(n, jax.ShapeDtypeStruct if ready else pltpu.VMEM)
    rows = [toks // cut] * cut + [toks] * (n - 1)
    out_shape = [jax.ShapeDtypeStruct((r, 2 * rank), jnp.float32) for r in rows]
    out_shape += [jax.ShapeDtypeStruct(a.shape, a.dtype) for a in far]
    if after:
        out_shape += buffers(len(after), jax.ShapeDtypeStruct)
    first, scratch = len(out_shape), own
    if ready:
        out_shape, scratch = out_shape + own, []
    hbm, vmem = pl.BlockSpec(memory_space=pltpu.HBM), pl.BlockSpec(memory_space=pltpu.VMEM)
    given = [pltpu.with_memory_space_constraint(a, pltpu.HBM) for a in (*arrays, *far)]
    stage = (flips, cut, after, len(ready) // 2, len(far))
    outs = pl.pallas_call(
        functools.partial(coords_kernel, stage),
        out_shape=out_shape,
        in_specs=[hbm] * len(given) + [vmem] * len(ready),
        out_specs=[vmem] * len(out_shape),
        input_output_aliases={len(given) + i: first + i for i in range(len(ready))},
        scratch_shapes=scratch
        + [
            pltpu.VMEM((n, toks, 2 * rank), jnp.float32),
            pltpu.SemaphoreType.DMA((n * chunks,)),
            pltpu.SemaphoreType.DMA((n * chunks,)),
            pltpu.SemaphoreType.DMA((2,)),
            pltpu.SemaphoreType.DMA,
        ],
        compiler_params=pltpu.CompilerParams(vmem_limit_bytes=VMEM_LIMIT),
        cost_estimate=pl.CostEstimate(
            flops=2 * n * toks * rank * (width + feats),
            bytes_accessed=n * (toks + rank) * (width + feats) * 2,
            transcendentals=0,
        ),
    )(*given, *ready)
    return outs[:first]


def halves_swapped(x):
    return pltpu.roll(x, x.shape[1] // 2, 1)


def lower_lanes(x):
    return lax.broadcasted_iota(jnp.int32, x.shape, 1) < x.shape[1] // 2


def pack_kernel(mine, core, packed):
    half = mine.shape[0] // 2
    first = mine[:half] + core[:half]
    second = mine[half:] + core[half:]
    low = lower_lanes(first)
    out = jnp.where(low, first, halves_swapped(second))
    inn = jnp.where(low, halves_swapped(first), second)
    coarse = inn.astype(packed.dtype)
    packed[:half] = out.astype(packed.dtype)
    packed[half : 2 * half] = coarse
    packed[2 * half :] = (inn - coarse.astype(jnp.float32)).astype(packed.dtype)


def pack(mine, core):
    toks, lanes = mine.shape
    vmem = pl.BlockSpec(memory_space=pltpu.VMEM)
    return pl.pallas_call(
        pack_kernel,
        out_shape=jax.ShapeDtypeStruct((3 * toks // 2, lanes), jnp.bfloat16),
        in_specs=[vmem] * 2,
        out_specs=vmem,
        compiler_params=pltpu.CompilerParams(vmem_limit_bytes=8 * 1024 * 1024),
    )(mine, core)


def grad_kernel(rank, mine, core_first, core_second, chip, grad, tmp):
    half = mine.shape[0] // 2
    out = chip[:half].astype(jnp.float32)
    inn = chip[half : 2 * half].astype(jnp.float32) + chip[2 * half :].astype(jnp.float32)
    low = lower_lanes(out)
    first = mine[:half] + core_first[...] + jnp.where(low, out, halves_swapped(inn))
    second = mine[half:] + core_second[...] + jnp.where(low, halves_swapped(out), inn)
    total = jnp.concatenate([first, second], axis=0)
    square = lax.dot_general(
        total,
        total,
        (((0,), (0,)), ((), ())),
        precision=lax.Precision.HIGHEST,
        preferred_element_type=jnp.float32,
    )
    tmp[...] = square[:rank, rank:]
    even = tmp[pl.ds(0, rank // 2, stride=2), :]
    odd = tmp[pl.ds(1, rank // 2, stride=2), :]
    flat = jnp.concatenate([even, odd], axis=1).astype(grad.dtype)
    for d in range(grad.shape[0]):
        grad[d] = flat


def layer_grad(mine, core, chip, copies):
    rank = mine.shape[1] // 2
    vmem = pl.BlockSpec(memory_space=pltpu.VMEM)
    return pl.pallas_call(
        functools.partial(grad_kernel, rank),
        out_shape=jax.ShapeDtypeStruct((copies, rank // 2, 2 * rank), jnp.bfloat16),
        in_specs=[vmem] * 4,
        out_specs=vmem,
        scratch_shapes=[pltpu.VMEM((rank, rank), jnp.float32)],
        compiler_params=pltpu.CompilerParams(vmem_limit_bytes=8 * 1024 * 1024),
    )(mine, *core, chip)


def one_layer_each(hidden_input, out_cotangent, in_projection, out_projection, forget_grads):
    docs, tensor = lax.axis_size("dp"), lax.axis_size("tensor")

    def swap(array, flip):
        return lax.ppermute(array, "tensor", [(i, i ^ flip) for i in range(tensor)])

    arrays = (hidden_input, out_cotangent, in_projection, out_projection)
    far_other, far_mine, *ready = coords((3, 2), arrays, after=(1, 0))
    far_sum = pack(far_mine, swap(far_other, 1))
    far_sum, ready = lax.optimization_barrier((far_sum, ready))
    chip = swap(far_sum, 2)
    *near_other, mine, forget_grads = coords(
        (1, 0), arrays, cut=2, ready=ready, far=(forget_grads,)
    )
    core = [swap(part, 1) for part in near_other]
    grad = layer_grad(mine, core, chip, docs)
    grads = lax.all_to_all(grad, "dp", 0, 0, tiled=True)
    part = lax.dot_general(
        grads.reshape(docs, -1),
        forget_grads,
        (((1,), (1,)), ((), ())),
        preferred_element_type=jnp.float32,
    )
    rows = jnp.broadcast_to(part[:, None, None, :], (docs, tensor, 1, part.shape[1]))
    rows = rows.reshape(docs * tensor, 1, part.shape[1])
    rows = lax.all_to_all(rows, ("dp", "tensor"), 0, 0, tiled=True)
    return rows.reshape(docs, tensor, -1).sum(axis=1).reshape(1, -1)


def any_split(hidden_input, out_cotangent, in_projection, out_projection, forget_grads):
    docs_axis = lax.axis_size("dp")
    in_coords = jnp.einsum(
        "ltf,lrf->tlr", hidden_input, in_projection, preferred_element_type=jnp.float32
    )
    out_coords = jnp.einsum(
        "ltf,lrf->tlr", out_cotangent, out_projection, preferred_element_type=jnp.float32
    )
    toks, layers, rank = in_coords.shape
    docs = toks // SEQ
    out_coords, in_coords = lax.psum((out_coords, in_coords), "tensor")
    grads = jnp.einsum(
        "dslr,dslc->dlrc",
        out_coords.reshape(docs, SEQ, layers, rank),
        in_coords.reshape(docs, SEQ, layers, rank),
        precision=lax.Precision.HIGHEST,
    ).reshape(docs, layers * rank * rank)
    width = grads.shape[1] // lax.axis_size("tensor")
    grads = lax.dynamic_slice_in_dim(grads, lax.axis_index("tensor") * width, width, 1)
    grads = lax.all_gather(grads.astype(jnp.bfloat16), "dp", axis=0, tiled=True)
    part = lax.dot_general(
        grads, forget_grads, (((1,), (1,)), ((), ())), preferred_element_type=jnp.float32
    )
    part = lax.psum(part, "tensor").reshape(docs_axis, docs, -1)
    rows = lax.all_to_all(part, "dp", 0, 0, tiled=True)
    return rows.transpose(1, 0, 2).reshape(docs, -1)


def solution(mesh):
    in_specs = (
        P(None, "dp", "tensor"),
        P(None, "dp", "tensor"),
        P(None, None, "tensor"),
        P(None, None, "tensor"),
        P("dp", "tensor"),
    )

    def on_device(hidden_input, *others):
        layers, toks, _ = hidden_input.shape
        single = mesh.shape["tensor"] == layers == 4 and toks == SEQ
        return (one_layer_each if single else any_split)(hidden_input, *others)

    return jax.shard_map(
        on_device, mesh=mesh, in_specs=in_specs, out_specs=P("dp", None), check_vma=False
    )
```

```python
import functools

import jax
import jax.numpy as jnp
from jax import lax
from jax.experimental import pallas as pl
from jax.experimental.pallas import tpu as pltpu
from jax.sharding import PartitionSpec as P

SEQ = 512
VMEM_LIMIT = 20 * 1024 * 1024


def pieces(lo, hi, split):
    before = (lo, min(hi, split), 0) if lo < split else None
    after = (max(lo, split) - split, hi - split, max(lo, split) - lo) if hi > split else None
    return before, after


def coords_kernel(stage, *refs):
    flips, cut, after, loaded, fetch = stage
    n, refs = len(flips), list(refs)
    hid, cot, inp, outp = refs[:4]
    far = refs[4] if fetch else None
    refs = refs[4 + fetch + 2 * loaded :]
    outs, refs = refs[: n + cut - 1], refs[n + cut - 1 :]
    near, refs = (refs[0], refs[1:]) if fetch else (None, refs)
    nextx, nextw, refs = (refs[0], refs[1], refs[2:]) if after else (None, None, refs)
    xbuf, wbuf, acc, xsem, wsem, nsem, fsem = refs
    rank = inp.shape[1]
    wide = xbuf.shape[2]
    chunks = (hid.shape[2] + cot.shape[2]) // wide
    me = lax.axis_index("tensor")
    parts = [pieces(c * wide, (c + 1) * wide, hid.shape[2]) for c in range(chunks)]

    def load(flip, c, x_at, w_at, x_sem, w_sem):
        layer = lax.bitwise_xor(me, flip)
        for part, x, w, row in zip(parts[c], (hid, cot), (inp, outp), (rank, 0)):
            if part is not None:
                src, dst = pl.ds(part[0], part[1] - part[0]), pl.ds(part[2], part[1] - part[0])
                pltpu.make_async_copy(
                    w.at[layer, :, src], w_at.at[pl.ds(row, rank), dst], w_sem
                ).start()
                pltpu.make_async_copy(x.at[layer, :, src], x_at.at[:, dst], x_sem).start()

    def clear(c, w_at):
        for part, row in zip(parts[c], (0, rank)):
            if part is not None:
                size = part[1] - part[0]
                w_at[row : row + rank, part[2] : part[2] + size] = jnp.zeros((rank, size), w_at.dtype)

    def arrived(x_at, w_at, x_sem, w_sem):
        w_all = w_at.at[pl.ds(0, rank)]
        pltpu.make_async_copy(w_all, w_all, w_sem).wait()
        pltpu.make_async_copy(x_at, x_at, x_sem).wait()

    steps = [(flip, c) for flip in flips for c in range(chunks)]
    for t, (flip, c) in enumerate(steps):
        if t >= loaded:
            load(flip, c, xbuf.at[t], wbuf.at[t], xsem.at[t], wsem.at[t])
    if after:
        load(after[0], 0, nextx.at[0], nextw.at[0], nsem.at[0], nsem.at[1])
    if fetch:
        pltpu.make_async_copy(far, near, fsem).start()
    for t, (flip, c) in enumerate(steps):
        if t >= loaded:
            clear(c, wbuf.at[t])
    if after:
        clear(0, nextw.at[0])
    acc[...] = jnp.zeros_like(acc)

    @pl.loop(0, len(steps))
    def _(t):
        @pl.when(t >= loaded)
        def _():
            arrived(xbuf.at[t], wbuf.at[t], xsem.at[t], wsem.at[t])

        acc[t // chunks] += lax.dot_general(
            xbuf[t], wbuf[t], (((1,), (1,)), ((), ())), preferred_element_type=jnp.float32
        )

    for k in range(cut):
        rows = outs[k].shape[0]
        outs[k][...] = acc[0, k * rows : (k + 1) * rows]
    for s in range(1, n):
        outs[cut + s - 1][...] = acc[s]
    if after:
        arrived(nextx.at[0], nextw.at[0], nsem.at[0], nsem.at[1])
    if fetch:
        pltpu.make_async_copy(far, near, fsem).wait()


def coords(flips, arrays, cut=1, after=(), ready=(), far=()):
    hid, cot, inp, _ = arrays
    n, chunks = len(flips), 2
    _, toks, width = hid.shape
    feats, rank = cot.shape[2], inp.shape[1]
    wide = (width + feats) // chunks

    def buffers(layers, make):
        steps = layers * chunks
        return [make((steps, rows, wide), jnp.bfloat16) for rows in (toks, 2 * rank)]

    own = buffers(n, jax.ShapeDtypeStruct if ready else pltpu.VMEM)
    rows = [toks // cut] * cut + [toks] * (n - 1)
    out_shape = [jax.ShapeDtypeStruct((r, 2 * rank), jnp.float32) for r in rows]
    out_shape += [jax.ShapeDtypeStruct(a.shape, a.dtype) for a in far]
    if after:
        out_shape += buffers(len(after), jax.ShapeDtypeStruct)
    first, scratch = len(out_shape), own
    if ready:
        out_shape, scratch = out_shape + own, []
    hbm, vmem = pl.BlockSpec(memory_space=pltpu.HBM), pl.BlockSpec(memory_space=pltpu.VMEM)
    given = [pltpu.with_memory_space_constraint(a, pltpu.HBM) for a in (*arrays, *far)]
    stage = (flips, cut, after, len(ready) // 2, len(far))
    outs = pl.pallas_call(
        functools.partial(coords_kernel, stage),
        out_shape=out_shape,
        in_specs=[hbm] * len(given) + [vmem] * len(ready),
        out_specs=[vmem] * len(out_shape),
        input_output_aliases={len(given) + i: first + i for i in range(len(ready))},
        scratch_shapes=scratch
        + [
            pltpu.VMEM((n, toks, 2 * rank), jnp.float32),
            pltpu.SemaphoreType.DMA((n * chunks,)),
            pltpu.SemaphoreType.DMA((n * chunks,)),
            pltpu.SemaphoreType.DMA((2,)),
            pltpu.SemaphoreType.DMA,
        ],
        compiler_params=pltpu.CompilerParams(vmem_limit_bytes=VMEM_LIMIT),
        cost_estimate=pl.CostEstimate(
            flops=2 * n * toks * rank * (width + feats),
            bytes_accessed=n * (toks + rank) * (width + feats) * 2,
            transcendentals=0,
        ),
    )(*given, *ready)
    return outs[:first]


def halves_swapped(x):
    return pltpu.roll(x, x.shape[1] // 2, 1)


def lower_lanes(x):
    return lax.broadcasted_iota(jnp.int32, x.shape, 1) < x.shape[1] // 2


def pack_kernel(mine, core, packed):
    half = mine.shape[0] // 2
    first = mine[:half] + core[:half]
    second = mine[half:] + core[half:]
    low = lower_lanes(first)
    out = jnp.where(low, first, halves_swapped(second))
    inn = jnp.where(low, halves_swapped(first), second)
    coarse = inn.astype(packed.dtype)
    packed[:half] = out.astype(packed.dtype)
    packed[half : 2 * half] = coarse
    packed[2 * half :] = (inn - coarse.astype(jnp.float32)).astype(packed.dtype)


def pack(mine, core):
    toks, lanes = mine.shape
    vmem = pl.BlockSpec(memory_space=pltpu.VMEM)
    return pl.pallas_call(
        pack_kernel,
        out_shape=jax.ShapeDtypeStruct((3 * toks // 2, lanes), jnp.bfloat16),
        in_specs=[vmem] * 2,
        out_specs=vmem,
        compiler_params=pltpu.CompilerParams(vmem_limit_bytes=8 * 1024 * 1024),
    )(mine, core)


def grad_kernel(rank, mine, core_first, core_second, chip, grad, tmp):
    half = mine.shape[0] // 2
    out = chip[:half].astype(jnp.float32)
    inn = chip[half : 2 * half].astype(jnp.float32) + chip[2 * half :].astype(jnp.float32)
    low = lower_lanes(out)
    first = mine[:half] + core_first[...] + jnp.where(low, out, halves_swapped(inn))
    second = mine[half:] + core_second[...] + jnp.where(low, halves_swapped(out), inn)
    total = jnp.concatenate([first, second], axis=0)
    coarse = total.astype(jnp.bfloat16)
    fine = (total - coarse.astype(jnp.float32)).astype(jnp.bfloat16)

    def product(x, y):
        return lax.dot_general(x, y, (((0,), (0,)), ((), ())), preferred_element_type=jnp.float32)

    square = product(coarse, coarse) + (product(coarse, fine) + product(fine, coarse))
    tmp[...] = square[:rank, rank:]
    even = tmp[pl.ds(0, rank // 2, stride=2), :]
    odd = tmp[pl.ds(1, rank // 2, stride=2), :]
    flat = jnp.concatenate([even, odd], axis=1).astype(grad.dtype)
    for d in range(grad.shape[0]):
        grad[d] = flat


def layer_grad(mine, core, chip, copies):
    rank = mine.shape[1] // 2
    vmem = pl.BlockSpec(memory_space=pltpu.VMEM)
    return pl.pallas_call(
        functools.partial(grad_kernel, rank),
        out_shape=jax.ShapeDtypeStruct((copies, rank // 2, 2 * rank), jnp.bfloat16),
        in_specs=[vmem] * 4,
        out_specs=vmem,
        scratch_shapes=[pltpu.VMEM((rank, rank), jnp.float32)],
        compiler_params=pltpu.CompilerParams(vmem_limit_bytes=8 * 1024 * 1024),
    )(mine, *core, chip)


def one_layer_each(hidden_input, out_cotangent, in_projection, out_projection, forget_grads):
    docs, tensor = lax.axis_size("dp"), lax.axis_size("tensor")

    def swap(array, flip):
        return lax.ppermute(array, "tensor", [(i, i ^ flip) for i in range(tensor)])

    arrays = (hidden_input, out_cotangent, in_projection, out_projection)
    far_other, far_mine, *ready = coords((3, 2), arrays, after=(1, 0))
    far_sum = pack(far_mine, swap(far_other, 1))
    far_sum, ready = lax.optimization_barrier((far_sum, ready))
    chip = swap(far_sum, 2)
    *near_other, mine, forget_grads = coords(
        (1, 0), arrays, cut=2, ready=ready, far=(forget_grads,)
    )
    core = [swap(part, 1) for part in near_other]
    grad = layer_grad(mine, core, chip, docs)
    grads = lax.all_to_all(grad, "dp", 0, 0, tiled=True)
    part = lax.dot_general(
        grads.reshape(docs, -1),
        forget_grads,
        (((1,), (1,)), ((), ())),
        preferred_element_type=jnp.float32,
    )
    rows = jnp.broadcast_to(part[:, None, None, :], (docs, tensor, 1, part.shape[1]))
    rows = rows.reshape(docs * tensor, 1, part.shape[1])
    rows = lax.all_to_all(rows, ("dp", "tensor"), 0, 0, tiled=True)
    return rows.reshape(docs, tensor, -1).sum(axis=1).reshape(1, -1)


def any_split(hidden_input, out_cotangent, in_projection, out_projection, forget_grads):
    docs_axis = lax.axis_size("dp")
    in_coords = jnp.einsum(
        "ltf,lrf->tlr", hidden_input, in_projection, preferred_element_type=jnp.float32
    )
    out_coords = jnp.einsum(
        "ltf,lrf->tlr", out_cotangent, out_projection, preferred_element_type=jnp.float32
    )
    toks, layers, rank = in_coords.shape
    docs = toks // SEQ
    out_coords, in_coords = lax.psum((out_coords, in_coords), "tensor")
    grads = jnp.einsum(
        "dslr,dslc->dlrc",
        out_coords.reshape(docs, SEQ, layers, rank),
        in_coords.reshape(docs, SEQ, layers, rank),
        precision=lax.Precision.HIGHEST,
    ).reshape(docs, layers * rank * rank)
    width = grads.shape[1] // lax.axis_size("tensor")
    grads = lax.dynamic_slice_in_dim(grads, lax.axis_index("tensor") * width, width, 1)
    grads = lax.all_gather(grads.astype(jnp.bfloat16), "dp", axis=0, tiled=True)
    part = lax.dot_general(
        grads, forget_grads, (((1,), (1,)), ((), ())), preferred_element_type=jnp.float32
    )
    part = lax.psum(part, "tensor").reshape(docs_axis, docs, -1)
    rows = lax.all_to_all(part, "dp", 0, 0, tiled=True)
    return rows.transpose(1, 0, 2).reshape(docs, -1)


def solution(mesh):
    in_specs = (
        P(None, "dp", "tensor"),
        P(None, "dp", "tensor"),
        P(None, None, "tensor"),
        P(None, None, "tensor"),
        P("dp", "tensor"),
    )

    def on_device(hidden_input, *others):
        layers, toks, _ = hidden_input.shape
        single = mesh.shape["tensor"] == layers == 4 and toks == SEQ
        return (one_layer_each if single else any_split)(hidden_input, *others)

    return jax.shard_map(
        on_device, mesh=mesh, in_specs=in_specs, out_specs=P("dp", None), check_vma=False
    )
```

```python
import functools

import jax
import jax.numpy as jnp
from jax import lax
from jax.experimental import pallas as pl
from jax.experimental.pallas import tpu as pltpu
from jax.sharding import PartitionSpec as P

SEQ = 512
VMEM_LIMIT = 20 * 1024 * 1024


def pieces(lo, hi, split):
    before = (lo, min(hi, split), 0) if lo < split else None
    after = (max(lo, split) - split, hi - split, max(lo, split) - lo) if hi > split else None
    return before, after


def coords_kernel(stage, *refs):
    flips, cut, after, loaded, fetch = stage
    halfway = loaded
    n, refs = len(flips), list(refs)
    hid, cot, inp, outp = refs[:4]
    far = refs[4] if fetch else None
    refs = refs[4 + fetch + 2 * loaded :]
    outs, refs = refs[: n + cut - 1], refs[n + cut - 1 :]
    near, refs = (refs[0], refs[1:]) if fetch else (None, refs)
    nextx, nextw, refs = (refs[0], refs[1], refs[2:]) if after else (None, None, refs)
    xbuf, wbuf, acc, xsem, wsem, nsem, fsem = refs
    rank = inp.shape[1]
    wide = xbuf.shape[2]
    chunks = (hid.shape[2] + cot.shape[2]) // wide
    me = lax.axis_index("tensor")
    parts = [pieces(c * wide, (c + 1) * wide, hid.shape[2]) for c in range(chunks)]

    def load(flip, c, x_at, w_at, x_sem, w_sem, skip=None):
        layer = lax.bitwise_xor(me, flip)
        for part, x, w, row in zip(parts[c], (hid, cot), (inp, outp), (rank, 0)):
            if part is not None:
                src, dst = pl.ds(part[0], part[1] - part[0]), pl.ds(part[2], part[1] - part[0])
                pltpu.make_async_copy(
                    w.at[layer, :, src], w_at.at[pl.ds(row, rank), dst], w_sem
                ).start()
                if x is not skip:
                    pltpu.make_async_copy(x.at[layer, :, src], x_at.at[:, dst], x_sem).start()

    def clear(c, w_at):
        for part, row in zip(parts[c], (0, rank)):
            if part is not None:
                size = part[1] - part[0]
                w_at[row : row + rank, part[2] : part[2] + size] = jnp.zeros((rank, size), w_at.dtype)

    def arrived(x_at, w_at, x_sem, w_sem):
        w_all = w_at.at[pl.ds(0, rank)]
        pltpu.make_async_copy(w_all, w_all, w_sem).wait()
        pltpu.make_async_copy(x_at, x_at, x_sem).wait()

    steps = [(flip, c) for flip in flips for c in range(chunks)]
    for t, (flip, c) in enumerate(steps):
        if t >= loaded:
            skip = hid if t == halfway and loaded else None
            load(flip, c, xbuf.at[t], wbuf.at[t], xsem.at[t], wsem.at[t], skip)
    if after:
        load(after[0], 0, nextx.at[0], nextw.at[0], nsem.at[0], nsem.at[1])
    if fetch:
        pltpu.make_async_copy(far, near, fsem).start()
    for t, (flip, c) in enumerate(steps):
        if t >= loaded:
            clear(c, wbuf.at[t])
    if after:
        clear(0, nextw.at[0])
    acc[...] = jnp.zeros_like(acc)

    @pl.loop(0, len(steps))
    def _(t):
        if loaded:

            @pl.when(t == halfway)
            def _():
                rest = xbuf.at[t, :, pl.ds(parts[halfway % chunks][1][2], cot.shape[2])]
                arrived(rest, wbuf.at[t], xsem.at[t], wsem.at[t])

        @pl.when(t >= loaded + bool(loaded))
        def _():
            arrived(xbuf.at[t], wbuf.at[t], xsem.at[t], wsem.at[t])

        acc[t // chunks] += lax.dot_general(
            xbuf[t], wbuf[t], (((1,), (1,)), ((), ())), preferred_element_type=jnp.float32
        )

    for k in range(cut):
        rows = outs[k].shape[0]
        outs[k][...] = acc[0, k * rows : (k + 1) * rows]
    for s in range(1, n):
        outs[cut + s - 1][...] = acc[s]
    if after:
        arrived(nextx.at[0], nextw.at[0], nsem.at[0], nsem.at[1])
    if fetch:
        pltpu.make_async_copy(far, near, fsem).wait()


def coords(flips, arrays, cut=1, after=(), ready=(), far=()):
    hid, cot, inp, _ = arrays
    n, chunks = len(flips), 2
    _, toks, width = hid.shape
    feats, rank = cot.shape[2], inp.shape[1]
    wide = (width + feats) // chunks

    def buffers(layers, make):
        steps = layers * chunks
        return [make((steps, rows, wide), jnp.bfloat16) for rows in (toks, 2 * rank)]

    own = buffers(n, jax.ShapeDtypeStruct if ready else pltpu.VMEM)
    rows = [toks // cut] * cut + [toks] * (n - 1)
    out_shape = [jax.ShapeDtypeStruct((r, 2 * rank), jnp.float32) for r in rows]
    out_shape += [jax.ShapeDtypeStruct(a.shape, a.dtype) for a in far]
    if after:
        out_shape += buffers(len(after), jax.ShapeDtypeStruct)
    first, scratch = len(out_shape), own
    if ready:
        out_shape, scratch = out_shape + own, []
    hbm, vmem = pl.BlockSpec(memory_space=pltpu.HBM), pl.BlockSpec(memory_space=pltpu.VMEM)
    given = [pltpu.with_memory_space_constraint(a, pltpu.HBM) for a in (*arrays, *far)]
    stage = (flips, cut, after, len(ready) // 2, len(far))
    outs = pl.pallas_call(
        functools.partial(coords_kernel, stage),
        out_shape=out_shape,
        in_specs=[hbm] * len(given) + [vmem] * len(ready),
        out_specs=[vmem] * len(out_shape),
        input_output_aliases={len(given) + i: first + i for i in range(len(ready))},
        scratch_shapes=scratch
        + [
            pltpu.VMEM((n, toks, 2 * rank), jnp.float32),
            pltpu.SemaphoreType.DMA((n * chunks,)),
            pltpu.SemaphoreType.DMA((n * chunks,)),
            pltpu.SemaphoreType.DMA((2,)),
            pltpu.SemaphoreType.DMA,
        ],
        compiler_params=pltpu.CompilerParams(vmem_limit_bytes=VMEM_LIMIT),
        cost_estimate=pl.CostEstimate(
            flops=2 * n * toks * rank * (width + feats),
            bytes_accessed=n * (toks + rank) * (width + feats) * 2,
            transcendentals=0,
        ),
    )(*given, *ready)
    return outs[:first]


def ahead_kernel(flip, hid, _, xbuf, sem):
    wide = xbuf.shape[2]
    size = hid.shape[2] - wide
    layer = lax.bitwise_xor(lax.axis_index("tensor"), flip)
    copy = pltpu.make_async_copy(
        hid.at[layer, :, pl.ds(wide, size)], xbuf.at[1, :, pl.ds(0, size)], sem
    )
    copy.start()
    copy.wait()


def ahead(flip, hid, xbuf):
    hbm, vmem = pl.BlockSpec(memory_space=pltpu.HBM), pl.BlockSpec(memory_space=pltpu.VMEM)
    return pl.pallas_call(
        functools.partial(ahead_kernel, flip),
        out_shape=jax.ShapeDtypeStruct(xbuf.shape, xbuf.dtype),
        in_specs=[hbm, vmem],
        out_specs=vmem,
        input_output_aliases={1: 0},
        scratch_shapes=[pltpu.SemaphoreType.DMA],
        compiler_params=pltpu.CompilerParams(vmem_limit_bytes=8 * 1024 * 1024),
        cost_estimate=pl.CostEstimate(flops=0, bytes_accessed=hid.size // 4, transcendentals=0),
    )(pltpu.with_memory_space_constraint(hid, pltpu.HBM), xbuf)


def halves_swapped(x):
    return pltpu.roll(x, x.shape[1] // 2, 1)


def lower_lanes(x):
    return lax.broadcasted_iota(jnp.int32, x.shape, 1) < x.shape[1] // 2


def pack_kernel(mine, core, packed):
    half = mine.shape[0] // 2
    first = mine[:half] + core[:half]
    second = mine[half:] + core[half:]
    low = lower_lanes(first)
    out = jnp.where(low, first, halves_swapped(second))
    inn = jnp.where(low, halves_swapped(first), second)
    coarse = inn.astype(packed.dtype)
    packed[:half] = out.astype(packed.dtype)
    packed[half : 2 * half] = coarse
    kept = packed.shape[0] - 2 * half
    packed[2 * half :] = (inn - coarse.astype(jnp.float32))[:kept].astype(packed.dtype)


def pack(mine, core):
    toks, lanes = mine.shape
    vmem = pl.BlockSpec(memory_space=pltpu.VMEM)
    return pl.pallas_call(
        pack_kernel,
        out_shape=jax.ShapeDtypeStruct((11 * toks // 8, lanes), jnp.bfloat16),
        in_specs=[vmem] * 2,
        out_specs=vmem,
        compiler_params=pltpu.CompilerParams(vmem_limit_bytes=8 * 1024 * 1024),
    )(mine, core)


def grad_kernel(rank, mine, core_first, core_second, chip, grad, tmp):
    half = mine.shape[0] // 2
    out = chip[:half].astype(jnp.float32)
    inn = chip[half : 2 * half].astype(jnp.float32)
    fine = chip[2 * half :].astype(jnp.float32)
    kept = fine.shape[0]
    inn = jnp.concatenate([inn[:kept] + fine, inn[kept:]], axis=0)
    low = lower_lanes(out)
    first = mine[:half] + core_first[...] + jnp.where(low, out, halves_swapped(inn))
    second = mine[half:] + core_second[...] + jnp.where(low, halves_swapped(out), inn)
    total = jnp.concatenate([first, second], axis=0)
    coarse = total.astype(jnp.bfloat16)
    fine = (total - coarse.astype(jnp.float32)).astype(jnp.bfloat16)

    def product(x, y):
        return lax.dot_general(x, y, (((0,), (0,)), ((), ())), preferred_element_type=jnp.float32)

    square = product(coarse, coarse) + (product(coarse, fine) + product(fine, coarse))
    tmp[...] = square[:rank, rank:]
    even = tmp[pl.ds(0, rank // 2, stride=2), :]
    odd = tmp[pl.ds(1, rank // 2, stride=2), :]
    flat = jnp.concatenate([even, odd], axis=1).astype(grad.dtype)
    for d in range(grad.shape[0]):
        grad[d] = flat


def layer_grad(mine, core, chip, copies):
    rank = mine.shape[1] // 2
    vmem = pl.BlockSpec(memory_space=pltpu.VMEM)
    return pl.pallas_call(
        functools.partial(grad_kernel, rank),
        out_shape=jax.ShapeDtypeStruct((copies, rank // 2, 2 * rank), jnp.bfloat16),
        in_specs=[vmem] * 4,
        out_specs=vmem,
        scratch_shapes=[pltpu.VMEM((rank, rank), jnp.float32)],
        compiler_params=pltpu.CompilerParams(vmem_limit_bytes=8 * 1024 * 1024),
    )(mine, *core, chip)


def one_layer_each(hidden_input, out_cotangent, in_projection, out_projection, forget_grads):
    docs, tensor = lax.axis_size("dp"), lax.axis_size("tensor")

    def swap(array, flip):
        return lax.ppermute(array, "tensor", [(i, i ^ flip) for i in range(tensor)])

    arrays = (hidden_input, out_cotangent, in_projection, out_projection)
    far_other, far_mine, *ready = coords((3, 2), arrays, after=(1, 0))
    far_core = swap(far_other, 1)
    ready[0] = ahead(1, hidden_input, ready[0])
    far_sum = pack(far_mine, far_core)
    far_sum, ready = lax.optimization_barrier((far_sum, ready))
    chip = swap(far_sum, 2)
    *near_other, mine, forget_grads = coords(
        (1, 0), arrays, cut=2, ready=ready, far=(forget_grads,)
    )
    core = [swap(part, 1) for part in near_other]
    grad = layer_grad(mine, core, chip, docs)
    grads = lax.all_to_all(grad, "dp", 0, 0, tiled=True)
    part = lax.dot_general(
        grads.reshape(docs, -1),
        forget_grads,
        (((1,), (1,)), ((), ())),
        preferred_element_type=jnp.float32,
    )
    rows = jnp.broadcast_to(part[:, None, None, :], (docs, tensor, 1, part.shape[1]))
    rows = rows.reshape(docs * tensor, 1, part.shape[1])
    rows = lax.all_to_all(rows, ("dp", "tensor"), 0, 0, tiled=True)
    return rows.reshape(docs, tensor, -1).sum(axis=1).reshape(1, -1)


def any_split(hidden_input, out_cotangent, in_projection, out_projection, forget_grads):
    docs_axis = lax.axis_size("dp")
    in_coords = jnp.einsum(
        "ltf,lrf->tlr", hidden_input, in_projection, preferred_element_type=jnp.float32
    )
    out_coords = jnp.einsum(
        "ltf,lrf->tlr", out_cotangent, out_projection, preferred_element_type=jnp.float32
    )
    toks, layers, rank = in_coords.shape
    docs = toks // SEQ
    out_coords, in_coords = lax.psum((out_coords, in_coords), "tensor")
    grads = jnp.einsum(
        "dslr,dslc->dlrc",
        out_coords.reshape(docs, SEQ, layers, rank),
        in_coords.reshape(docs, SEQ, layers, rank),
        precision=lax.Precision.HIGHEST,
    ).reshape(docs, layers * rank * rank)
    width = grads.shape[1] // lax.axis_size("tensor")
    grads = lax.dynamic_slice_in_dim(grads, lax.axis_index("tensor") * width, width, 1)
    grads = lax.all_gather(grads.astype(jnp.bfloat16), "dp", axis=0, tiled=True)
    part = lax.dot_general(
        grads, forget_grads, (((1,), (1,)), ((), ())), preferred_element_type=jnp.float32
    )
    part = lax.psum(part, "tensor").reshape(docs_axis, docs, -1)
    rows = lax.all_to_all(part, "dp", 0, 0, tiled=True)
    return rows.transpose(1, 0, 2).reshape(docs, -1)


def solution(mesh):
    in_specs = (
        P(None, "dp", "tensor"),
        P(None, "dp", "tensor"),
        P(None, None, "tensor"),
        P(None, None, "tensor"),
        P("dp", "tensor"),
    )

    def on_device(hidden_input, *others):
        layers, toks, _ = hidden_input.shape
        single = mesh.shape["tensor"] == layers == 4 and toks == SEQ
        return (one_layer_each if single else any_split)(hidden_input, *others)

    return jax.shard_map(
        on_device, mesh=mesh, in_specs=in_specs, out_specs=P("dp", None), check_vma=False
    )
```

```python
import functools

import jax
import jax.numpy as jnp
from jax import lax
from jax.experimental import pallas as pl
from jax.experimental.pallas import tpu as pltpu
from jax.sharding import PartitionSpec as P

SEQ = 512
VMEM_LIMIT = 20 * 1024 * 1024


def pieces(lo, hi, split):
    before = (lo, min(hi, split), 0) if lo < split else None
    after = (max(lo, split) - split, hi - split, max(lo, split) - lo) if hi > split else None
    return before, after


def coords_kernel(stage, *refs):
    flips, cut, after, loaded, partly, fetch = stage
    halfway = loaded
    n, refs = len(flips), list(refs)
    hid, cot, inp, outp = refs[:4]
    far = refs[4] if fetch else None
    refs = refs[4 + fetch + 2 * loaded :]
    outs, refs = refs[: n + cut - 1], refs[n + cut - 1 :]
    near, refs = (refs[0], refs[1:]) if fetch else (None, refs)
    nextx, nextw, refs = (refs[0], refs[1], refs[2:]) if after else (None, None, refs)
    xbuf, wbuf, acc, xsem, wsem, nsem, fsem = refs
    rank = inp.shape[1]
    wide = xbuf.shape[2]
    chunks = (hid.shape[2] + cot.shape[2]) // wide
    me = lax.axis_index("tensor")
    parts = [pieces(c * wide, (c + 1) * wide, hid.shape[2]) for c in range(chunks)]

    def load(flip, c, x_at, w_at, x_sem, w_sem, skip=None):
        layer = lax.bitwise_xor(me, flip)
        for part, x, w, row in zip(parts[c], (hid, cot), (inp, outp), (rank, 0)):
            if part is not None:
                src, dst = pl.ds(part[0], part[1] - part[0]), pl.ds(part[2], part[1] - part[0])
                pltpu.make_async_copy(
                    w.at[layer, :, src], w_at.at[pl.ds(row, rank), dst], w_sem
                ).start()
                if x is not skip:
                    pltpu.make_async_copy(x.at[layer, :, src], x_at.at[:, dst], x_sem).start()

    def clear(c, w_at):
        for part, row in zip(parts[c], (0, rank)):
            if part is not None:
                size = part[1] - part[0]
                w_at[row : row + rank, part[2] : part[2] + size] = jnp.zeros((rank, size), w_at.dtype)

    def arrived(x_at, w_at, x_sem, w_sem):
        w_all = w_at.at[pl.ds(0, rank)]
        pltpu.make_async_copy(w_all, w_all, w_sem).wait()
        pltpu.make_async_copy(x_at, x_at, x_sem).wait()

    steps = [(flip, c) for flip in flips for c in range(chunks)]
    for t, (flip, c) in enumerate(steps):
        if t >= loaded:
            skip = hid if t == halfway and partly else None
            load(flip, c, xbuf.at[t], wbuf.at[t], xsem.at[t], wsem.at[t], skip)
    if after:
        load(after[0], 0, nextx.at[0], nextw.at[0], nsem.at[0], nsem.at[1])
    if fetch:
        pltpu.make_async_copy(far, near, fsem).start()
    for t, (flip, c) in enumerate(steps):
        if t >= loaded:
            clear(c, wbuf.at[t])
    if after:
        clear(0, nextw.at[0])
    acc[...] = jnp.zeros_like(acc)

    @pl.loop(0, len(steps))
    def _(t):
        if partly:

            @pl.when(t == halfway)
            def _():
                rest = xbuf.at[t, :, pl.ds(parts[halfway % chunks][1][2], cot.shape[2])]
                arrived(rest, wbuf.at[t], xsem.at[t], wsem.at[t])

        @pl.when(t >= loaded + partly)
        def _():
            arrived(xbuf.at[t], wbuf.at[t], xsem.at[t], wsem.at[t])

        acc[t // chunks] += lax.dot_general(
            xbuf[t], wbuf[t], (((1,), (1,)), ((), ())), preferred_element_type=jnp.float32
        )

    for k in range(cut):
        rows = outs[k].shape[0]
        outs[k][...] = acc[0, k * rows : (k + 1) * rows]
    for s in range(1, n):
        outs[cut + s - 1][...] = acc[s]
    if after:
        arrived(nextx.at[0], nextw.at[0], nsem.at[0], nsem.at[1])
    if fetch:
        pltpu.make_async_copy(far, near, fsem).wait()


def coords(flips, arrays, cut=1, after=(), ready=(), partly=False, far=()):
    hid, cot, inp, _ = arrays
    n, chunks = len(flips), 2
    _, toks, width = hid.shape
    feats, rank = cot.shape[2], inp.shape[1]
    wide = (width + feats) // chunks

    def buffers(layers, make):
        steps = layers * chunks
        return [make((steps, rows, wide), jnp.bfloat16) for rows in (toks, 2 * rank)]

    own = buffers(n, jax.ShapeDtypeStruct if ready else pltpu.VMEM)
    rows = [toks // cut] * cut + [toks] * (n - 1)
    out_shape = [jax.ShapeDtypeStruct((r, 2 * rank), jnp.float32) for r in rows]
    out_shape += [jax.ShapeDtypeStruct(a.shape, a.dtype) for a in far]
    if after:
        out_shape += buffers(len(after), jax.ShapeDtypeStruct)
    first, scratch = len(out_shape), own
    if ready:
        out_shape, scratch = out_shape + own, []
    hbm, vmem = pl.BlockSpec(memory_space=pltpu.HBM), pl.BlockSpec(memory_space=pltpu.VMEM)
    given = [pltpu.with_memory_space_constraint(a, pltpu.HBM) for a in (*arrays, *far)]
    stage = (flips, cut, after, len(ready) // 2, partly, len(far))
    outs = pl.pallas_call(
        functools.partial(coords_kernel, stage),
        out_shape=out_shape,
        in_specs=[hbm] * len(given) + [vmem] * len(ready),
        out_specs=[vmem] * len(out_shape),
        input_output_aliases={len(given) + i: first + i for i in range(len(ready))},
        scratch_shapes=scratch
        + [
            pltpu.VMEM((n, toks, 2 * rank), jnp.float32),
            pltpu.SemaphoreType.DMA((n * chunks,)),
            pltpu.SemaphoreType.DMA((n * chunks,)),
            pltpu.SemaphoreType.DMA((2,)),
            pltpu.SemaphoreType.DMA,
        ],
        compiler_params=pltpu.CompilerParams(vmem_limit_bytes=VMEM_LIMIT),
        cost_estimate=pl.CostEstimate(
            flops=2 * n * toks * rank * (width + feats),
            bytes_accessed=n * (toks + rank) * (width + feats) * 2,
            transcendentals=0,
        ),
    )(*given, *ready)
    return outs[:first]


def ahead_kernel(flip, hid, _, xbuf, sem):
    wide = xbuf.shape[2]
    size = hid.shape[2] - wide
    layer = lax.bitwise_xor(lax.axis_index("tensor"), flip)
    copy = pltpu.make_async_copy(
        hid.at[layer, :, pl.ds(wide, size)], xbuf.at[1, :, pl.ds(0, size)], sem
    )
    copy.start()
    copy.wait()


def ahead(flip, hid, xbuf):
    hbm, vmem = pl.BlockSpec(memory_space=pltpu.HBM), pl.BlockSpec(memory_space=pltpu.VMEM)
    return pl.pallas_call(
        functools.partial(ahead_kernel, flip),
        out_shape=jax.ShapeDtypeStruct(xbuf.shape, xbuf.dtype),
        in_specs=[hbm, vmem],
        out_specs=vmem,
        input_output_aliases={1: 0},
        scratch_shapes=[pltpu.SemaphoreType.DMA],
        compiler_params=pltpu.CompilerParams(vmem_limit_bytes=8 * 1024 * 1024),
        cost_estimate=pl.CostEstimate(flops=0, bytes_accessed=hid.size // 4, transcendentals=0),
    )(pltpu.with_memory_space_constraint(hid, pltpu.HBM), xbuf)


def product(x, y):
    return lax.dot_general(x, y, (((0,), (0,)), ((), ())), preferred_element_type=jnp.float32)


def pack_kernel(rank, mine, core, packed):
    toks = mine.shape[0]
    total = mine[...] + core[...]
    coarse = total.astype(packed.dtype)
    fine = (total - coarse.astype(jnp.float32)).astype(packed.dtype)
    packed[:toks] = coarse
    lost = product(fine, coarse) + product(coarse, fine)
    packed[toks:] = lost[:rank].astype(packed.dtype)


def pack(mine, core):
    toks, lanes = mine.shape
    vmem = pl.BlockSpec(memory_space=pltpu.VMEM)
    return pl.pallas_call(
        functools.partial(pack_kernel, lanes // 2),
        out_shape=jax.ShapeDtypeStruct((toks + lanes // 2, lanes), jnp.bfloat16),
        in_specs=[vmem] * 2,
        out_specs=vmem,
        compiler_params=pltpu.CompilerParams(vmem_limit_bytes=8 * 1024 * 1024),
    )(mine, core)


def grad_kernel(rank, mine, core_first, core_second, chip, grad, tmp):
    toks = mine.shape[0]
    core = jnp.concatenate([core_first[...], core_second[...]], axis=0)
    total = mine[...] + core + chip[:toks].astype(jnp.float32)
    coarse = total.astype(jnp.bfloat16)
    fine = (total - coarse.astype(jnp.float32)).astype(jnp.bfloat16)
    square = product(coarse, coarse) + (product(coarse, fine) + product(fine, coarse))
    tmp[...] = (square[:rank] + chip[toks:].astype(jnp.float32))[:, rank:]
    even = tmp[pl.ds(0, rank // 2, stride=2), :]
    odd = tmp[pl.ds(1, rank // 2, stride=2), :]
    flat = jnp.concatenate([even, odd], axis=1).astype(grad.dtype)
    for d in range(grad.shape[0]):
        grad[d] = flat


def layer_grad(mine, core, chip, copies):
    rank = mine.shape[1] // 2
    vmem = pl.BlockSpec(memory_space=pltpu.VMEM)
    return pl.pallas_call(
        functools.partial(grad_kernel, rank),
        out_shape=jax.ShapeDtypeStruct((copies, rank // 2, 2 * rank), jnp.bfloat16),
        in_specs=[vmem] * 4,
        out_specs=vmem,
        scratch_shapes=[pltpu.VMEM((rank, rank), jnp.float32)],
        compiler_params=pltpu.CompilerParams(vmem_limit_bytes=8 * 1024 * 1024),
    )(mine, *core, chip)


def one_layer_each(hidden_input, out_cotangent, in_projection, out_projection, forget_grads):
    docs, tensor = lax.axis_size("dp"), lax.axis_size("tensor")

    def swap(array, flip):
        return lax.ppermute(array, "tensor", [(i, i ^ flip) for i in range(tensor)])

    arrays = (hidden_input, out_cotangent, in_projection, out_projection)
    far_other, far_mine, *ready = coords((3, 2), arrays, after=(1,))
    far_core = swap(far_other, 1)
    ready[0] = ahead(1, hidden_input, ready[0])
    far_sum = pack(far_mine, far_core)
    far_sum, ready = lax.optimization_barrier((far_sum, ready))
    chip = swap(far_sum, 2)
    *near_other, next_x, next_w = coords(
        (1,), arrays, cut=2, after=(0,), ready=ready, partly=True
    )
    core = [swap(part, 1) for part in near_other]
    mine, forget_grads = coords((0,), arrays, ready=(next_x, next_w), far=(forget_grads,))
    grad = layer_grad(mine, core, chip, docs)
    grads = lax.all_to_all(grad, "dp", 0, 0, tiled=True)
    part = lax.dot_general(
        grads.reshape(docs, -1),
        forget_grads,
        (((1,), (1,)), ((), ())),
        preferred_element_type=jnp.float32,
    )
    rows = jnp.broadcast_to(part[:, None, None, :], (docs, tensor, 1, part.shape[1]))
    rows = rows.reshape(docs * tensor, 1, part.shape[1])
    rows = lax.all_to_all(rows, ("dp", "tensor"), 0, 0, tiled=True)
    return rows.reshape(docs, tensor, -1).sum(axis=1).reshape(1, -1)


def any_split(hidden_input, out_cotangent, in_projection, out_projection, forget_grads):
    docs_axis = lax.axis_size("dp")
    in_coords = jnp.einsum(
        "ltf,lrf->tlr", hidden_input, in_projection, preferred_element_type=jnp.float32
    )
    out_coords = jnp.einsum(
        "ltf,lrf->tlr", out_cotangent, out_projection, preferred_element_type=jnp.float32
    )
    toks, layers, rank = in_coords.shape
    docs = toks // SEQ
    out_coords, in_coords = lax.psum((out_coords, in_coords), "tensor")
    grads = jnp.einsum(
        "dslr,dslc->dlrc",
        out_coords.reshape(docs, SEQ, layers, rank),
        in_coords.reshape(docs, SEQ, layers, rank),
        precision=lax.Precision.HIGHEST,
    ).reshape(docs, layers * rank * rank)
    width = grads.shape[1] // lax.axis_size("tensor")
    grads = lax.dynamic_slice_in_dim(grads, lax.axis_index("tensor") * width, width, 1)
    grads = lax.all_gather(grads.astype(jnp.bfloat16), "dp", axis=0, tiled=True)
    part = lax.dot_general(
        grads, forget_grads, (((1,), (1,)), ((), ())), preferred_element_type=jnp.float32
    )
    part = lax.psum(part, "tensor").reshape(docs_axis, docs, -1)
    rows = lax.all_to_all(part, "dp", 0, 0, tiled=True)
    return rows.transpose(1, 0, 2).reshape(docs, -1)


def solution(mesh):
    in_specs = (
        P(None, "dp", "tensor"),
        P(None, "dp", "tensor"),
        P(None, None, "tensor"),
        P(None, None, "tensor"),
        P("dp", "tensor"),
    )

    def on_device(hidden_input, *others):
        layers, toks, _ = hidden_input.shape
        single = mesh.shape["tensor"] == layers == 4 and toks == SEQ
        return (one_layer_each if single else any_split)(hidden_input, *others)

    return jax.shard_map(
        on_device, mesh=mesh, in_specs=in_specs, out_specs=P("dp", None), check_vma=False
    )
```

```python
import functools

import jax
import jax.numpy as jnp
from jax import lax
from jax.experimental import pallas as pl
from jax.experimental.pallas import tpu as pltpu
from jax.sharding import PartitionSpec as P

SEQ = 512
VMEM_LIMIT = 20 * 1024 * 1024


def pieces(lo, hi, split):
    before = (lo, min(hi, split), 0) if lo < split else None
    after = (max(lo, split) - split, hi - split, max(lo, split) - lo) if hi > split else None
    return before, after


def coords_kernel(stage, *refs):
    flips, cut, after, loaded, partly, fetch = stage
    halfway = loaded
    n, refs = len(flips), list(refs)
    hid, cot, inp, outp = refs[:4]
    far = refs[4] if fetch else None
    refs = refs[4 + fetch + 2 * loaded :]
    outs, refs = refs[: n + cut - 1], refs[n + cut - 1 :]
    near, refs = (refs[0], refs[1:]) if fetch else (None, refs)
    nextx, nextw, refs = (refs[0], refs[1], refs[2:]) if after else (None, None, refs)
    xbuf, wbuf, acc, xsem, wsem, nsem, fsem = refs
    rank = inp.shape[1]
    wide = xbuf.shape[2]
    chunks = (hid.shape[2] + cot.shape[2]) // wide
    me = lax.axis_index("tensor")
    parts = [pieces(c * wide, (c + 1) * wide, hid.shape[2]) for c in range(chunks)]

    def load(flip, c, x_at, w_at, x_sem, w_sem, skip=None):
        layer = lax.bitwise_xor(me, flip)
        for part, x, w, row in zip(parts[c], (hid, cot), (inp, outp), (rank, 0)):
            if part is not None:
                src, dst = pl.ds(part[0], part[1] - part[0]), pl.ds(part[2], part[1] - part[0])
                pltpu.make_async_copy(
                    w.at[layer, :, src], w_at.at[pl.ds(row, rank), dst], w_sem
                ).start()
                if x is not skip:
                    pltpu.make_async_copy(x.at[layer, :, src], x_at.at[:, dst], x_sem).start()

    def clear(c, w_at):
        for part, row in zip(parts[c], (0, rank)):
            if part is not None:
                size = part[1] - part[0]
                w_at[row : row + rank, part[2] : part[2] + size] = jnp.zeros((rank, size), w_at.dtype)

    def arrived(x_at, w_at, x_sem, w_sem):
        w_all = w_at.at[pl.ds(0, rank)]
        pltpu.make_async_copy(w_all, w_all, w_sem).wait()
        pltpu.make_async_copy(x_at, x_at, x_sem).wait()

    steps = [(flip, c) for flip in flips for c in range(chunks)]
    for t, (flip, c) in enumerate(steps):
        if t >= loaded:
            skip = hid if t == halfway and partly else None
            load(flip, c, xbuf.at[t], wbuf.at[t], xsem.at[t], wsem.at[t], skip)
    if after:
        load(after[0], 0, nextx.at[0], nextw.at[0], nsem.at[0], nsem.at[1])
    if fetch:
        pltpu.make_async_copy(far, near, fsem).start()
    for t, (flip, c) in enumerate(steps):
        if t >= loaded:
            clear(c, wbuf.at[t])
    if after:
        clear(0, nextw.at[0])
    acc[...] = jnp.zeros_like(acc)

    @pl.loop(0, len(steps))
    def _(t):
        if partly:

            @pl.when(t == halfway)
            def _():
                rest = xbuf.at[t, :, pl.ds(parts[halfway % chunks][1][2], cot.shape[2])]
                arrived(rest, wbuf.at[t], xsem.at[t], wsem.at[t])

        @pl.when(t >= loaded + partly)
        def _():
            arrived(xbuf.at[t], wbuf.at[t], xsem.at[t], wsem.at[t])

        acc[t // chunks] += lax.dot_general(
            xbuf[t], wbuf[t], (((1,), (1,)), ((), ())), preferred_element_type=jnp.float32
        )

    for k in range(cut):
        rows = outs[k].shape[0]
        outs[k][...] = acc[0, k * rows : (k + 1) * rows]
    for s in range(1, n):
        outs[cut + s - 1][...] = acc[s]
    if after:
        arrived(nextx.at[0], nextw.at[0], nsem.at[0], nsem.at[1])
    if fetch:
        pltpu.make_async_copy(far, near, fsem).wait()


def coords(flips, arrays, cut=1, after=(), ready=(), partly=False, far=()):
    hid, cot, inp, _ = arrays
    n, chunks = len(flips), 2
    _, toks, width = hid.shape
    feats, rank = cot.shape[2], inp.shape[1]
    wide = (width + feats) // chunks

    def buffers(layers, make):
        steps = layers * chunks
        return [make((steps, rows, wide), jnp.bfloat16) for rows in (toks, 2 * rank)]

    own = buffers(n, jax.ShapeDtypeStruct if ready else pltpu.VMEM)
    rows = [toks // cut] * cut + [toks] * (n - 1)
    out_shape = [jax.ShapeDtypeStruct((r, 2 * rank), jnp.float32) for r in rows]
    out_shape += [jax.ShapeDtypeStruct(a.shape, a.dtype) for a in far]
    if after:
        out_shape += buffers(len(after), jax.ShapeDtypeStruct)
    first, scratch = len(out_shape), own
    if ready:
        out_shape, scratch = out_shape + own, []
    hbm, vmem = pl.BlockSpec(memory_space=pltpu.HBM), pl.BlockSpec(memory_space=pltpu.VMEM)
    given = [pltpu.with_memory_space_constraint(a, pltpu.HBM) for a in (*arrays, *far)]
    stage = (flips, cut, after, len(ready) // 2, partly, len(far))
    outs = pl.pallas_call(
        functools.partial(coords_kernel, stage),
        out_shape=out_shape,
        in_specs=[hbm] * len(given) + [vmem] * len(ready),
        out_specs=[vmem] * len(out_shape),
        input_output_aliases={len(given) + i: first + i for i in range(len(ready))},
        scratch_shapes=scratch
        + [
            pltpu.VMEM((n, toks, 2 * rank), jnp.float32),
            pltpu.SemaphoreType.DMA((n * chunks,)),
            pltpu.SemaphoreType.DMA((n * chunks,)),
            pltpu.SemaphoreType.DMA((2,)),
            pltpu.SemaphoreType.DMA,
        ],
        compiler_params=pltpu.CompilerParams(vmem_limit_bytes=VMEM_LIMIT),
        cost_estimate=pl.CostEstimate(
            flops=2 * n * toks * rank * (width + feats),
            bytes_accessed=n * (toks + rank) * (width + feats) * 2,
            transcendentals=0,
        ),
    )(*given, *ready)
    return outs[:first]


def ahead_kernel(flip, hid, _, xbuf, sem):
    wide = xbuf.shape[2]
    size = hid.shape[2] - wide
    layer = lax.bitwise_xor(lax.axis_index("tensor"), flip)
    copy = pltpu.make_async_copy(
        hid.at[layer, :, pl.ds(wide, size)], xbuf.at[1, :, pl.ds(0, size)], sem
    )
    copy.start()
    copy.wait()


def ahead(flip, hid, xbuf):
    hbm, vmem = pl.BlockSpec(memory_space=pltpu.HBM), pl.BlockSpec(memory_space=pltpu.VMEM)
    return pl.pallas_call(
        functools.partial(ahead_kernel, flip),
        out_shape=jax.ShapeDtypeStruct(xbuf.shape, xbuf.dtype),
        in_specs=[hbm, vmem],
        out_specs=vmem,
        input_output_aliases={1: 0},
        scratch_shapes=[pltpu.SemaphoreType.DMA],
        compiler_params=pltpu.CompilerParams(vmem_limit_bytes=8 * 1024 * 1024),
        cost_estimate=pl.CostEstimate(flops=0, bytes_accessed=hid.size // 4, transcendentals=0),
    )(pltpu.with_memory_space_constraint(hid, pltpu.HBM), xbuf)


def product(x, y):
    return lax.dot_general(x, y, (((0,), (0,)), ((), ())), preferred_element_type=jnp.float32)


def pack_kernel(rank, mine, core, packed):
    toks = mine.shape[0]
    total = mine[...] + core[...]
    coarse = total.astype(packed.dtype)
    fine = (total - coarse.astype(jnp.float32)).astype(packed.dtype)
    packed[:toks] = coarse
    lost = product(fine[:, :rank], coarse) + product(coarse[:, :rank], fine)
    packed[toks:] = lost.astype(packed.dtype)


def pack(mine, core):
    toks, lanes = mine.shape
    vmem = pl.BlockSpec(memory_space=pltpu.VMEM)
    return pl.pallas_call(
        functools.partial(pack_kernel, lanes // 2),
        out_shape=jax.ShapeDtypeStruct((toks + lanes // 2, lanes), jnp.bfloat16),
        in_specs=[vmem] * 2,
        out_specs=vmem,
        compiler_params=pltpu.CompilerParams(vmem_limit_bytes=8 * 1024 * 1024),
    )(mine, core)


def grad_kernel(rank, mine, core_first, core_second, chip, grad, tmp):
    toks = mine.shape[0]
    core = jnp.concatenate([core_first[...], core_second[...]], axis=0)
    total = mine[...] + core + chip[:toks].astype(jnp.float32)
    coarse = total.astype(jnp.bfloat16)
    fine = (total - coarse.astype(jnp.float32)).astype(jnp.bfloat16)
    left, rest = coarse[:, :rank], fine[:, :rank]
    grads = product(left, coarse) + (product(left, fine) + product(rest, coarse))
    tmp[...] = (grads + chip[toks:].astype(jnp.float32))[:, rank:]
    even = tmp[pl.ds(0, rank // 2, stride=2), :]
    odd = tmp[pl.ds(1, rank // 2, stride=2), :]
    flat = jnp.concatenate([even, odd], axis=1).astype(grad.dtype)
    for d in range(grad.shape[0]):
        grad[d] = flat


def layer_grad(mine, core, chip, copies):
    rank = mine.shape[1] // 2
    vmem = pl.BlockSpec(memory_space=pltpu.VMEM)
    return pl.pallas_call(
        functools.partial(grad_kernel, rank),
        out_shape=jax.ShapeDtypeStruct((copies, rank // 2, 2 * rank), jnp.bfloat16),
        in_specs=[vmem] * 4,
        out_specs=vmem,
        scratch_shapes=[pltpu.VMEM((rank, rank), jnp.float32)],
        compiler_params=pltpu.CompilerParams(vmem_limit_bytes=8 * 1024 * 1024),
    )(mine, *core, chip)


def one_layer_each(hidden_input, out_cotangent, in_projection, out_projection, forget_grads):
    docs, tensor = lax.axis_size("dp"), lax.axis_size("tensor")

    def swap(array, flip):
        return lax.ppermute(array, "tensor", [(i, i ^ flip) for i in range(tensor)])

    arrays = (hidden_input, out_cotangent, in_projection, out_projection)
    far_other, far_mine, *ready = coords((3, 2), arrays, after=(1,))
    far_core = swap(far_other, 1)
    ready[0] = ahead(1, hidden_input, ready[0])
    far_sum = pack(far_mine, far_core)
    far_sum, ready = lax.optimization_barrier((far_sum, ready))
    chip = swap(far_sum, 2)
    *near_other, next_x, next_w = coords(
        (1,), arrays, cut=2, after=(0,), ready=ready, partly=True
    )
    core = [swap(part, 1) for part in near_other]
    mine, forget_grads = coords((0,), arrays, ready=(next_x, next_w), far=(forget_grads,))
    grad = layer_grad(mine, core, chip, docs)
    grads = lax.all_to_all(grad, "dp", 0, 0, tiled=True)
    part = lax.dot_general(
        grads.reshape(docs, -1),
        forget_grads,
        (((1,), (1,)), ((), ())),
        preferred_element_type=jnp.float32,
    )
    rows = jnp.broadcast_to(part[:, None, None, :], (docs, tensor, 1, part.shape[1]))
    rows = rows.reshape(docs * tensor, 1, part.shape[1])
    rows = lax.all_to_all(rows, ("dp", "tensor"), 0, 0, tiled=True)
    return rows.reshape(docs, tensor, -1).sum(axis=1).reshape(1, -1)


def any_split(hidden_input, out_cotangent, in_projection, out_projection, forget_grads):
    docs_axis = lax.axis_size("dp")
    in_coords = jnp.einsum(
        "ltf,lrf->tlr", hidden_input, in_projection, preferred_element_type=jnp.float32
    )
    out_coords = jnp.einsum(
        "ltf,lrf->tlr", out_cotangent, out_projection, preferred_element_type=jnp.float32
    )
    toks, layers, rank = in_coords.shape
    docs = toks // SEQ
    out_coords, in_coords = lax.psum((out_coords, in_coords), "tensor")
    grads = jnp.einsum(
        "dslr,dslc->dlrc",
        out_coords.reshape(docs, SEQ, layers, rank),
        in_coords.reshape(docs, SEQ, layers, rank),
        precision=lax.Precision.HIGHEST,
    ).reshape(docs, layers * rank * rank)
    width = grads.shape[1] // lax.axis_size("tensor")
    grads = lax.dynamic_slice_in_dim(grads, lax.axis_index("tensor") * width, width, 1)
    grads = lax.all_gather(grads.astype(jnp.bfloat16), "dp", axis=0, tiled=True)
    part = lax.dot_general(
        grads, forget_grads, (((1,), (1,)), ((), ())), preferred_element_type=jnp.float32
    )
    part = lax.psum(part, "tensor").reshape(docs_axis, docs, -1)
    rows = lax.all_to_all(part, "dp", 0, 0, tiled=True)
    return rows.transpose(1, 0, 2).reshape(docs, -1)


def solution(mesh):
    in_specs = (
        P(None, "dp", "tensor"),
        P(None, "dp", "tensor"),
        P(None, None, "tensor"),
        P(None, None, "tensor"),
        P("dp", "tensor"),
    )

    def on_device(hidden_input, *others):
        layers, toks, _ = hidden_input.shape
        single = mesh.shape["tensor"] == layers == 4 and toks == SEQ
        return (one_layer_each if single else any_split)(hidden_input, *others)

    return jax.shard_map(
        on_device, mesh=mesh, in_specs=in_specs, out_specs=P("dp", None), check_vma=False
    )
```

```python
import functools

import jax
import jax.numpy as jnp
from jax import lax
from jax.experimental import pallas as pl
from jax.experimental.pallas import tpu as pltpu
from jax.sharding import PartitionSpec as P

SEQ = 512
VMEM_LIMIT = 20 * 1024 * 1024


def pieces(lo, hi, split):
    before = (lo, min(hi, split), 0) if lo < split else None
    after = (max(lo, split) - split, hi - split, max(lo, split) - lo) if hi > split else None
    return before, after


def coords_kernel(stage, *refs):
    flips, cut, after, loaded, partly, fetch = stage
    halfway = loaded
    n, refs = len(flips), list(refs)
    hid, cot, inp, outp = refs[:4]
    far = refs[4] if fetch else None
    refs = refs[4 + fetch + 2 * loaded :]
    outs, refs = refs[: n + cut - 1], refs[n + cut - 1 :]
    near, refs = (refs[0], refs[1:]) if fetch else (None, refs)
    nextx, nextw, refs = (refs[0], refs[1], refs[2:]) if after else (None, None, refs)
    xbuf, wbuf, acc, xsem, wsem, nsem, fsem = refs
    rank = inp.shape[1]
    wide = xbuf.shape[2]
    chunks = (hid.shape[2] + cot.shape[2]) // wide
    me = lax.axis_index("tensor")
    parts = [pieces(c * wide, (c + 1) * wide, hid.shape[2]) for c in range(chunks)]

    def load(flip, c, x_at, w_at, x_sem, w_sem, skip=None):
        layer = lax.bitwise_xor(me, flip)
        for part, x, w, row in zip(parts[c], (hid, cot), (inp, outp), (rank, 0)):
            if part is not None:
                src, dst = pl.ds(part[0], part[1] - part[0]), pl.ds(part[2], part[1] - part[0])
                pltpu.make_async_copy(
                    w.at[layer, :, src], w_at.at[pl.ds(row, rank), dst], w_sem
                ).start()
                if x is not skip:
                    pltpu.make_async_copy(x.at[layer, :, src], x_at.at[:, dst], x_sem).start()

    def clear(c, w_at):
        for part, row in zip(parts[c], (0, rank)):
            if part is not None:
                size = part[1] - part[0]
                w_at[row : row + rank, part[2] : part[2] + size] = jnp.zeros((rank, size), w_at.dtype)

    def arrived(x_at, w_at, x_sem, w_sem):
        w_all = w_at.at[pl.ds(0, rank)]
        pltpu.make_async_copy(w_all, w_all, w_sem).wait()
        pltpu.make_async_copy(x_at, x_at, x_sem).wait()

    steps = [(flip, c) for flip in flips for c in range(chunks)]
    for t, (flip, c) in enumerate(steps):
        if t >= loaded:
            skip = hid if t == halfway and partly else None
            load(flip, c, xbuf.at[t], wbuf.at[t], xsem.at[t], wsem.at[t], skip)
    if after:
        load(after[0], 0, nextx.at[0], nextw.at[0], nsem.at[0], nsem.at[1])
    if fetch:
        pltpu.make_async_copy(far, near, fsem).start()
    for t, (flip, c) in enumerate(steps):
        if t >= loaded:
            clear(c, wbuf.at[t])
    if after:
        clear(0, nextw.at[0])
    acc[...] = jnp.zeros_like(acc)

    @pl.loop(0, len(steps))
    def _(t):
        if partly:

            @pl.when(t == halfway)
            def _():
                rest = xbuf.at[t, :, pl.ds(parts[halfway % chunks][1][2], cot.shape[2])]
                arrived(rest, wbuf.at[t], xsem.at[t], wsem.at[t])

        @pl.when(t >= loaded + partly)
        def _():
            arrived(xbuf.at[t], wbuf.at[t], xsem.at[t], wsem.at[t])

        acc[t // chunks] += lax.dot_general(
            xbuf[t], wbuf[t], (((1,), (1,)), ((), ())), preferred_element_type=jnp.float32
        )

    for k in range(cut):
        rows = outs[k].shape[0]
        outs[k][...] = acc[0, k * rows : (k + 1) * rows]
    for s in range(1, n):
        outs[cut + s - 1][...] = acc[s]
    if after:
        arrived(nextx.at[0], nextw.at[0], nsem.at[0], nsem.at[1])
    if fetch:
        pltpu.make_async_copy(far, near, fsem).wait()


def coords(flips, arrays, cut=1, after=(), ready=(), partly=False, far=()):
    hid, cot, inp, _ = arrays
    n, chunks = len(flips), 2
    _, toks, width = hid.shape
    feats, rank = cot.shape[2], inp.shape[1]
    wide = (width + feats) // chunks

    def buffers(layers, make):
        steps = layers * chunks
        return [make((steps, rows, wide), jnp.bfloat16) for rows in (toks, 2 * rank)]

    own = buffers(n, jax.ShapeDtypeStruct if ready else pltpu.VMEM)
    rows = [toks // cut] * cut + [toks] * (n - 1)
    out_shape = [jax.ShapeDtypeStruct((r, 2 * rank), jnp.float32) for r in rows]
    out_shape += [jax.ShapeDtypeStruct(a.shape, a.dtype) for a in far]
    if after:
        out_shape += buffers(len(after), jax.ShapeDtypeStruct)
    first, scratch = len(out_shape), own
    if ready:
        out_shape, scratch = out_shape + own, []
    hbm, vmem = pl.BlockSpec(memory_space=pltpu.HBM), pl.BlockSpec(memory_space=pltpu.VMEM)
    given = [pltpu.with_memory_space_constraint(a, pltpu.HBM) for a in (*arrays, *far)]
    stage = (flips, cut, after, len(ready) // 2, partly, len(far))
    outs = pl.pallas_call(
        functools.partial(coords_kernel, stage),
        out_shape=out_shape,
        in_specs=[hbm] * len(given) + [vmem] * len(ready),
        out_specs=[vmem] * len(out_shape),
        input_output_aliases={len(given) + i: first + i for i in range(len(ready))},
        scratch_shapes=scratch
        + [
            pltpu.VMEM((n, toks, 2 * rank), jnp.float32),
            pltpu.SemaphoreType.DMA((n * chunks,)),
            pltpu.SemaphoreType.DMA((n * chunks,)),
            pltpu.SemaphoreType.DMA((2,)),
            pltpu.SemaphoreType.DMA,
        ],
        compiler_params=pltpu.CompilerParams(vmem_limit_bytes=VMEM_LIMIT),
        cost_estimate=pl.CostEstimate(
            flops=2 * n * toks * rank * (width + feats),
            bytes_accessed=n * (toks + rank) * (width + feats) * 2,
            transcendentals=0,
        ),
    )(*given, *ready)
    return outs[:first]


def ahead_kernel(flip, hid, _, xbuf, sem):
    wide = xbuf.shape[2]
    size = hid.shape[2] - wide
    layer = lax.bitwise_xor(lax.axis_index("tensor"), flip)
    copy = pltpu.make_async_copy(
        hid.at[layer, :, pl.ds(wide, size)], xbuf.at[1, :, pl.ds(0, size)], sem
    )
    copy.start()
    copy.wait()


def ahead(flip, hid, xbuf):
    hbm, vmem = pl.BlockSpec(memory_space=pltpu.HBM), pl.BlockSpec(memory_space=pltpu.VMEM)
    return pl.pallas_call(
        functools.partial(ahead_kernel, flip),
        out_shape=jax.ShapeDtypeStruct(xbuf.shape, xbuf.dtype),
        in_specs=[hbm, vmem],
        out_specs=vmem,
        input_output_aliases={1: 0},
        scratch_shapes=[pltpu.SemaphoreType.DMA],
        compiler_params=pltpu.CompilerParams(vmem_limit_bytes=8 * 1024 * 1024),
        cost_estimate=pl.CostEstimate(flops=0, bytes_accessed=hid.size // 4, transcendentals=0),
    )(pltpu.with_memory_space_constraint(hid, pltpu.HBM), xbuf)


def product(x, y):
    return lax.dot_general(x, y, (((0,), (0,)), ((), ())), preferred_element_type=jnp.float32)


def pack_kernel(rank, mine, core, packed):
    toks = mine.shape[0]
    total = mine[...] + core[...]
    coarse = total.astype(packed.dtype)
    fine = (total - coarse.astype(jnp.float32)).astype(packed.dtype)
    packed[:toks] = coarse
    lost = product(fine[:, :rank], coarse) + product(coarse[:, :rank], fine)
    packed[toks:] = lost.astype(packed.dtype)


def pack(mine, core):
    toks, lanes = mine.shape
    vmem = pl.BlockSpec(memory_space=pltpu.VMEM)
    return pl.pallas_call(
        functools.partial(pack_kernel, lanes // 2),
        out_shape=jax.ShapeDtypeStruct((toks + lanes // 2, lanes), jnp.bfloat16),
        in_specs=[vmem] * 2,
        out_specs=vmem,
        compiler_params=pltpu.CompilerParams(vmem_limit_bytes=8 * 1024 * 1024),
    )(mine, core)


def grad_kernel(rank, mine, core_first, core_second, chip, grad, tmp):
    toks = mine.shape[0]
    core = jnp.concatenate([core_first[...], core_second[...]], axis=0)
    total = mine[...] + core + chip[:toks].astype(jnp.float32)
    coarse = total.astype(jnp.bfloat16)
    fine = (total - coarse.astype(jnp.float32)).astype(jnp.bfloat16)
    left, rest = coarse[:, :rank], fine[:, :rank]
    grads = product(left, coarse) + (product(left, fine) + product(rest, coarse))
    tmp[...] = (grads + chip[toks:].astype(jnp.float32))[:, rank:]
    even = tmp[pl.ds(0, rank // 2, stride=2), :]
    odd = tmp[pl.ds(1, rank // 2, stride=2), :]
    flat = jnp.concatenate([even, odd], axis=1).astype(grad.dtype)
    for d in range(grad.shape[0]):
        grad[d] = flat


def layer_grad(mine, core, chip, copies):
    rank = mine.shape[1] // 2
    vmem = pl.BlockSpec(memory_space=pltpu.VMEM)
    return pl.pallas_call(
        functools.partial(grad_kernel, rank),
        out_shape=jax.ShapeDtypeStruct((copies, rank // 2, 2 * rank), jnp.bfloat16),
        in_specs=[vmem] * 4,
        out_specs=vmem,
        scratch_shapes=[pltpu.VMEM((rank, rank), jnp.float32)],
        compiler_params=pltpu.CompilerParams(vmem_limit_bytes=8 * 1024 * 1024),
    )(mine, *core, chip)


def one_layer_each(hidden_input, out_cotangent, in_projection, out_projection, forget_grads):
    docs, tensor = lax.axis_size("dp"), lax.axis_size("tensor")

    def swap(array, flip):
        return lax.ppermute(array, "tensor", [(i, i ^ flip) for i in range(tensor)])

    arrays = (hidden_input, out_cotangent, in_projection, out_projection)
    far_other, far_mine, *ready = coords((3, 2), arrays, after=(1, 0))
    far_core = swap(far_other, 1)
    ready[0] = ahead(1, hidden_input, ready[0])
    far_sum = pack(far_mine, far_core)
    far_sum, ready = lax.optimization_barrier((far_sum, ready))
    chip = swap(far_sum, 2)
    *near_other, mine, forget_grads = coords(
        (1, 0), arrays, cut=2, ready=ready, partly=True, far=(forget_grads,)
    )
    core = [swap(part, 1) for part in near_other]
    grad = layer_grad(mine, core, chip, docs)
    grads = lax.all_to_all(grad, "dp", 0, 0, tiled=True)
    part = lax.dot_general(
        grads.reshape(docs, -1),
        forget_grads,
        (((1,), (1,)), ((), ())),
        preferred_element_type=jnp.float32,
    )
    rows = jnp.broadcast_to(part[:, None, None, :], (docs, tensor, 1, part.shape[1]))
    rows = rows.reshape(docs * tensor, 1, part.shape[1])
    rows = lax.all_to_all(rows, ("dp", "tensor"), 0, 0, tiled=True)
    return rows.reshape(docs, tensor, -1).sum(axis=1).reshape(1, -1)


def any_split(hidden_input, out_cotangent, in_projection, out_projection, forget_grads):
    docs_axis = lax.axis_size("dp")
    in_coords = jnp.einsum(
        "ltf,lrf->tlr", hidden_input, in_projection, preferred_element_type=jnp.float32
    )
    out_coords = jnp.einsum(
        "ltf,lrf->tlr", out_cotangent, out_projection, preferred_element_type=jnp.float32
    )
    toks, layers, rank = in_coords.shape
    docs = toks // SEQ
    out_coords, in_coords = lax.psum((out_coords, in_coords), "tensor")
    grads = jnp.einsum(
        "dslr,dslc->dlrc",
        out_coords.reshape(docs, SEQ, layers, rank),
        in_coords.reshape(docs, SEQ, layers, rank),
        precision=lax.Precision.HIGHEST,
    ).reshape(docs, layers * rank * rank)
    width = grads.shape[1] // lax.axis_size("tensor")
    grads = lax.dynamic_slice_in_dim(grads, lax.axis_index("tensor") * width, width, 1)
    grads = lax.all_gather(grads.astype(jnp.bfloat16), "dp", axis=0, tiled=True)
    part = lax.dot_general(
        grads, forget_grads, (((1,), (1,)), ((), ())), preferred_element_type=jnp.float32
    )
    part = lax.psum(part, "tensor").reshape(docs_axis, docs, -1)
    rows = lax.all_to_all(part, "dp", 0, 0, tiled=True)
    return rows.transpose(1, 0, 2).reshape(docs, -1)


def solution(mesh):
    in_specs = (
        P(None, "dp", "tensor"),
        P(None, "dp", "tensor"),
        P(None, None, "tensor"),
        P(None, None, "tensor"),
        P("dp", "tensor"),
    )

    def on_device(hidden_input, *others):
        layers, toks, _ = hidden_input.shape
        single = mesh.shape["tensor"] == layers == 4 and toks == SEQ
        return (one_layer_each if single else any_split)(hidden_input, *others)

    return jax.shard_map(
        on_device, mesh=mesh, in_specs=in_specs, out_specs=P("dp", None), check_vma=False
    )
```
